32 devices in a mesh: dp: 16 (over z, x, core), seq: 2 (over y).
Axes of the slice: x: 2, y: 2, z: 4, core: 2. Of those that a mesh axis runs over, the one named last changes fastest.
Arguments:
- video: bfloat16 [16, 256, 3072], P('dp', 'seq'), may hold values from -6 to 6
- shift: float32 [16, 3072], P('dp'), may hold values from -5 to 5
- scale: float32 [16, 3072], P('dp'), may hold values from -2.5 to 2.5
- project_weight: bfloat16 [3, 3072, 2048], P(None, 'dp', 'seq'), may hold values from -0.109375 to 0.109375
- project_bias: float32 [3, 2048], P(None, 'seq'), may hold values from -3 to 3
- query_gain: float32 [128], replicated, may hold values from 0.5 to 12
- key_gain: float32 [128], replicated, may hold values from 0.5 to 12
- tile_table: int32 [16, 16, 12], P('dp'), may hold values from 0 to 15, as said below
Outputs:
- attended: bfloat16 [16, 256, 2048], P('dp', 'seq')
The draws below stay inside these ranges and needn't reach their ends.
Inputs may be any that keep to these rules, and one draw needn't show every extreme that they name: `tile_table`: for query tile t of frame f = t // 8, row (t % 8) // 4 and column t % 4 of the 2 x 4 grid of tiles of a frame, the entries are the tiles of 2 consecutive frames, both rows and 3 consecutive columns that contain t, listed with the frame changing slowest and the column fastest (slot s: frame step s // 6, row s % 6 // 3, column step s % 3); the window's placement varies from tile to tile.
All inputs are finite; a program needn't handle non-finite values.
Results may differ from the reference program's by a relative error of at most 0.005.
The reference program's roundings to bfloat16 on the way (of `normed`, `queries`, `keys`, `values` and `weights`) count: a program that leaves them out, or rounds other values in their place, can miss the bound.
Values may be sent and summed in bfloat16 or wider, within the bound.
A program may use at most 128 MiB of HBM per device.

```python
import jax
import jax.numpy as jnp
from jax import lax

D = 3072
HEADS = 16
HD = 128
TILE = 16
SEQLEN = 256
NT = 16
VIDEOS = 16


def draw_query_gain(key, part):
    return jax.random.uniform(jax.random.fold_in(key, 11), (HD,), jnp.float32, 0.5, 1.5)


def draw_key_gain(key, part):
    return jax.random.uniform(jax.random.fold_in(key, 23), (HD,), jnp.float32, 0.5, 1.5)


def draw_tile_table(key, part):
    frames = NT // 8
    tiles = jnp.arange(NT, dtype=jnp.int32)
    frame_of = tiles // 8
    column_of = tiles % 4
    frame_low = jnp.maximum(frame_of - 1, 0)
    frame_high = jnp.minimum(frame_of, frames - 2)
    column_low = jnp.maximum(column_of - 2, 0)
    column_high = jnp.minimum(column_of, 1)
    frame_start = frame_low + jax.random.randint(jax.random.fold_in(key, 31), (VIDEOS, NT), 0, frame_high - frame_low + 1)
    column_start = column_low + jax.random.randint(jax.random.fold_in(key, 37), (VIDEOS, NT), 0, column_high - column_low + 1)
    slots = jnp.arange(12, dtype=jnp.int32)
    frame_step = slots // 6
    row_step = slots % 6 // 3
    column_step = slots % 3
    table = (frame_start[:, :, None] + frame_step) * 8 + row_step * 4 + column_start[:, :, None] + column_step
    return table.astype(jnp.int32)


def block_levels(key, extent, cuts, low, high):
    def one(position, blocks):
        draws = jax.random.uniform(jax.random.fold_in(jax.random.fold_in(key, 6), position), (blocks,), jnp.float32, low / len(cuts), high / len(cuts))
        return jnp.repeat(jnp.exp(draws), extent[position] // blocks).reshape((-1,) + (1,) * (len(extent) - position - 1))

    factor_of = one(*cuts[0])
    for cut in cuts[1:]:
        factor_of = factor_of * one(*cut)
    return factor_of


def centred(key, dims, scale, bound, shards=(), kind=jnp.bfloat16):
    entries = scale * jax.random.normal(key, dims, jnp.float32)
    if shards:
        entries = entries * block_levels(key, dims, shards, -0.22, 0.18)
    return jnp.clip(entries, -bound, bound).astype(kind)


def setup_inputs(seed: int = 0) -> dict:
    arg_keys = jax.random.split(jax.random.key(seed), 9)
    video = centred(arg_keys[0], (VIDEOS, SEQLEN, D), 1.0, 6.0, ((0, 16), (1, 2)))
    shift = centred(arg_keys[1], (VIDEOS, D), 1.0, 5.0, ((0, 16),), jnp.float32)
    scale = centred(arg_keys[2], (VIDEOS, D), 0.5, 2.5, ((0, 16),), jnp.float32)
    project_weight = centred(arg_keys[3], (3, D, HEADS * HD), D ** -0.5, 0.109375, ((1, 16), (2, 2)))
    project_bias = centred(arg_keys[4], (3, HEADS * HD), 0.5, 3.0, ((1, 2),), jnp.float32)
    query_gain = draw_query_gain(jax.random.fold_in(arg_keys[8], 71), 0)
    key_gain = draw_key_gain(jax.random.fold_in(arg_keys[8], 71), 0)
    tile_table = draw_tile_table(jax.random.fold_in(arg_keys[8], 71), 0)
    return {"video": video, "shift": shift, "scale": scale, "project_weight": project_weight, "project_bias": project_bias, "query_gain": query_gain, "key_gain": key_gain, "tile_table": tile_table}


EPS = 1e-06

def rms_norm(values_in, gain):
    return (values_in * lax.rsqrt(lax.optimization_barrier(jnp.mean(values_in * values_in, axis=-1, keepdims=True)) + EPS) * gain).astype(jnp.bfloat16)

def window_attention(queries, keys, values, table):
    seqlen, heads, width = queries.shape
    ntiles = seqlen // TILE
    ktiles = table.shape[1]
    query_tiles = queries.reshape(ntiles, TILE, heads, width).astype(jnp.float32)
    key_sel = jnp.take(keys.reshape(ntiles, TILE, heads, width), table, axis=0).reshape(ntiles, ktiles * TILE, heads, width)
    value_sel = jnp.take(values.reshape(ntiles, TILE, heads, width), table, axis=0).reshape(ntiles, ktiles * TILE, heads, width)
    scores = jnp.einsum('nqhd,nkhd->nhqk', query_tiles, key_sel.astype(jnp.float32)) * width ** (-0.5)
    largest = lax.optimization_barrier(jnp.max(scores, axis=-1, keepdims=True))
    expo = jnp.exp(scores - largest)
    weights = (expo / lax.optimization_barrier(jnp.sum(expo, axis=-1, keepdims=True))).astype(jnp.bfloat16)
    result = jnp.einsum('nhqk,nkhd->nqhd', weights.astype(jnp.float32), value_sel.astype(jnp.float32))
    return result.astype(jnp.bfloat16).reshape(seqlen, heads * width)

def one_video(video_one, shift_one, scale_one, table, project_weight, project_bias, query_gain, key_gain):
    tokens = video_one.astype(jnp.float32)
    centre = lax.optimization_barrier(jnp.mean(tokens, axis=-1, keepdims=True))
    spread = lax.optimization_barrier(jnp.mean((tokens - centre) ** 2, axis=-1, keepdims=True))
    normed = ((tokens - centre) * lax.rsqrt(spread + EPS) * (1.0 + scale_one) + shift_one).astype(jnp.bfloat16)
    seqlen = normed.shape[0]
    heads = project_weight.shape[2] // HD
    query = jnp.dot(normed, project_weight[0], preferred_element_type=jnp.float32) + project_bias[0]
    key = jnp.dot(normed, project_weight[1], preferred_element_type=jnp.float32) + project_bias[1]
    value = jnp.dot(normed, project_weight[2], preferred_element_type=jnp.float32) + project_bias[2]
    queries = rms_norm(query.reshape(seqlen, heads, HD), query_gain)
    keys = rms_norm(key.reshape(seqlen, heads, HD), key_gain)
    values = value.reshape(seqlen, heads, HD).astype(jnp.bfloat16)
    return window_attention(queries, keys, values, table)

def reference(video, shift, scale, project_weight, project_bias, query_gain, key_gain, tile_table):

    def step(items):
        return one_video(items[0], items[1], items[2], items[3], project_weight, project_bias, query_gain, key_gain)
    return lax.map(step, (video, shift, scale, tile_table))
```

```python
import jax
import jax.numpy as jnp
from jax import lax
from jax.experimental import pallas as pl
from jax.experimental.pallas import tpu as pltpu
from jax.sharding import PartitionSpec as P

HD = 128
TILE = 16
LANES = 128


EPS = 1e-06
MASKED = -1e30
CHUNKS = 2
MESH = pl.DeviceIdType.MESH


def rms_norm(values_in, gain):
    return (
        values_in * lax.rsqrt(jnp.mean(values_in * values_in, axis=-1, keepdims=True) + EPS) * gain
    ).astype(jnp.bfloat16)


def window_attention(projected, query_gain, key_gain, table):
    seqlen = projected.shape[1]
    heads = projected.shape[2] // HD
    ntiles = seqlen // TILE
    queries = rms_norm(projected[0].reshape(seqlen, heads, HD), query_gain)
    keys = rms_norm(projected[1].reshape(seqlen, heads, HD), key_gain)
    values = projected[2].reshape(seqlen, heads, HD).astype(jnp.bfloat16)
    member = jnp.any(table[:, :, None] == jnp.arange(ntiles, dtype=table.dtype), axis=1)
    seen = jnp.repeat(jnp.repeat(member, TILE, axis=0), TILE, axis=1)
    scores = jnp.einsum(
        "qhd,khd->hqk", queries, keys, preferred_element_type=jnp.float32
    ) * HD ** (-0.5)
    scores = jnp.where(seen[None], scores, MASKED)
    largest = jnp.max(scores, axis=-1, keepdims=True)
    expo = jnp.exp(scores - largest)
    weights = (expo / jnp.sum(expo, axis=-1, keepdims=True)).astype(jnp.bfloat16)
    result = jnp.einsum("hqk,khd->qhd", weights, values, preferred_element_type=jnp.float32)
    return result.astype(jnp.bfloat16).reshape(seqlen, heads * HD)


def gathered_device(video, shift, scale, project_weight, project_bias, query_gain, key_gain, tile_table):
    tokens = video[0].astype(jnp.float32)
    centre = jnp.mean(tokens, axis=-1, keepdims=True)
    spread = jnp.mean((tokens - centre) ** 2, axis=-1, keepdims=True)
    normed = ((tokens - centre) * lax.rsqrt(spread + EPS) * (1.0 + scale[0]) + shift[0]).astype(
        jnp.bfloat16
    )
    gathered = lax.all_gather(normed, "seq", axis=0, tiled=True)
    projected = jnp.einsum(
        "sd,tdc->tsc",
        gathered,
        lax.all_gather(project_weight, "dp", axis=1, tiled=True),
        preferred_element_type=jnp.float32,
    )
    projected = projected + project_bias[:, None, :]
    local_heads = window_attention(projected, query_gain, key_gain, tile_table[0])
    returned = lax.all_to_all(local_heads, "seq", split_axis=0, concat_axis=1, tiled=True)
    return returned[None]


def layer_kernel(
    video_hbm,
    shift_hbm,
    scale_hbm,
    member_ref,
    bias_hbm,
    qgain_hbm,
    kgain_hbm,
    weight_ref,
    out_ref,
    video_ref,
    shift_ref,
    scale_ref,
    bias_ref,
    qgain_ref,
    kgain_ref,
    wbuf,
    tok,
    obuf,
    own_sem,
    small_sem,
    wsend,
    zsend,
    wrecv,
    tsend,
    trecv,
    osend,
    orecv,
):
    dp = lax.axis_index("dp")
    y = lax.axis_index("seq")
    core = lax.rem(dp, 2)
    x = lax.rem(dp // 2, 2)
    z = dp // 4
    rows, width = video_ref.shape
    slab = weight_ref.shape[1]
    end = jnp.logical_or(z == 0, z == 3)
    inner = jnp.logical_not(end)
    mate = 1 + z // 3
    far = 3 * (z // 2)
    peer = 3 - z

    def pos(k):
        xk = 1 - x if k & 2 else x
        ck = 1 - core if k & 1 else core
        return xk * 2 + ck

    def at(k, flip=0, layer=None):
        return ((z if layer is None else layer) * 4 + pos(k), 1 - y if flip else y)

    small = [
        pltpu.make_async_copy(src, dst, small_sem.at[n])
        for n, (src, dst) in enumerate(
            [
                (video_hbm, video_ref),
                (shift_hbm, shift_ref),
                (scale_hbm, scale_ref),
                (bias_hbm, bias_ref),
                (qgain_hbm, qgain_ref),
                (kgain_hbm, kgain_ref),
            ]
        )
    ]

    barrier = pltpu.get_barrier_semaphore()

    def greet(target):
        pl.semaphore_signal(barrier, inc=1, device_id=target, device_id_type=MESH)

    for flip in range(2):
        for k in range(4):
            if k or flip:
                greet(at(k, flip))

    @pl.when(end)
    def _():
        for flip in range(2):
            for k in range(4):
                greet(at(k, flip, mate))

    @pl.when(inner)
    def _():
        for flip in range(2):
            for k in range(4):
                greet(at(k, flip, far))
        greet(at(0, 0, peer))

    def block(h, owner):
        return wbuf.at[h, pl.ds(pl.multiple_of(owner * slab, 16), slab), :]

    def columns(place, h):
        return pl.ds(pl.multiple_of((place * 2 + h) * HD, HD), HD)

    mine = pl.ds(pl.multiple_of(dp * slab, 16), slab)

    for h in range(2):
        for i in range(3):
            pltpu.make_async_copy(
                weight_ref.at[i, :, columns(pos(0), h)],
                wbuf.at[h, mine, pl.ds(i * HD, HD)],
                own_sem.at[h],
            ).start()
        if h == 0:
            for copy in small:
                copy.start()

    @pl.when(end)
    def _():
        pl.semaphore_wait(barrier, 15)

    @pl.when(inner)
    def _():
        pl.semaphore_wait(barrier, 16)

    def remote(src, dst, send, recv, target):
        return pltpu.make_async_remote_copy(
            src_ref=src,
            dst_ref=dst,
            send_sem=send,
            recv_sem=recv,
            device_id=target,
            device_id_type=MESH,
        )

    def piece_sends(h, k):
        return [
            remote(
                weight_ref.at[i, :, columns(pos(k), h)],
                wbuf.at[h, mine, pl.ds(i * HD, HD)],
                wsend.at[h, k - 1, i],
                wrecv.at[h, dp],
                at(k),
            )
            for i in range(3)
        ]

    def z_send(h, owner, way, layer):
        return remote(
            block(h, owner),
            block(h, owner),
            zsend.at[h, owner, way],
            wrecv.at[h, owner],
            at(0, 0, layer),
        )

    def wait_block(h, owner):
        remote(
            block(h, owner), block(h, owner), zsend.at[h, owner, 0], wrecv.at[h, owner], at(1)
        ).wait_recv()

    def wait_own(h, k):
        owner = z * 4 + pos(k)
        if k:
            wait_block(h, owner)
        else:
            pltpu.make_async_copy(block(h, owner), block(h, owner), own_sem.at[h]).wait()

    def ways(h, layer, role):
        if role == "end":
            return [(0, mate)] if layer is z else []
        if layer is peer or layer is far_peer:
            return [(0, far)] if h == 0 else []
        if layer is far:
            return [(1, peer)]
        return [(1, peer), (0, far)] if h == 0 else [(1, peer)]

    far_peer = 3 - far

    def pass_on(h, layer, k, role):
        for way, target in ways(h, layer, role):
            z_send(h, layer * 4 + pos(k), way, target).start()

    def own_layer(h, ks, role):
        for k in ks:
            wait_own(h, k)
            pass_on(h, z, k, role)

    def relay(h, layers, role):
        for k in range(4):
            for layer in layers:
                wait_block(h, layer * 4 + pos(k))
                pass_on(h, layer, k, role)

    for k in (2, 3, 1):
        for copy in piece_sends(0, k):
            copy.start()

    @pl.when(end)
    def _():
        own_layer(0, (0, 1), "end")

    @pl.when(inner)
    def _():
        own_layer(0, (0, 1), "inner")

    for copy in small:
        copy.wait()
    step = 16
    part = rows // CHUNKS

    def norm_chunk(q):
        half = pl.multiple_of(y * rows + q * part, TILE)

        @pl.loop(0, part // step)
        def _(n):
            first = pl.multiple_of(n * step, step)
            tokens = video_ref[pl.ds(q * part + first, step), :].astype(jnp.float32)
            centre = jnp.mean(tokens, axis=-1, keepdims=True)
            shifted = tokens - centre
            spread = jnp.mean(shifted * shifted, axis=-1, keepdims=True)
            normed = shifted * lax.rsqrt(spread + EPS) * (1.0 + scale_ref[...]) + shift_ref[...]
            tok[0, pos(0), pl.ds(half + first, step), 0:width] = normed.astype(jnp.bfloat16)

        tok[0, pos(0), pl.ds(half, part), width : width + LANES] = member_ref[
            q * part : (q + 1) * part, :
        ]

    def tokens_at(group, place, side, q):
        first = pl.multiple_of(side * rows + q * part, TILE)
        return tok.at[group, place, pl.ds(first, part), :]

    def token_send(n, group, place, side, q, target, to_group=None):
        to_group = group if to_group is None else to_group
        return remote(
            tokens_at(group, place, side, q),
            tokens_at(to_group, place, side, q),
            tsend.at[to_group, n, q],
            trecv.at[to_group, place, side, q],
            target,
        )

    def wait_tokens(group, place, side, q):
        token_send(0, group, place, side, q, at(1)).wait_recv()

    own, beside, across, diagonal = (
        (pos(0), y),
        (pos(2), y),
        (pos(0), 1 - y),
        (pos(2), 1 - y),
    )

    def own_tokens(q):
        return [
            token_send(0, 0, *own, q, at(2)),
            token_send(1, 0, *own, q, at(0, 1)),
            token_send(2, 0, *own, q, at(1)),
        ]

    def passed_tokens(q):
        return [
            token_send(3, 0, *beside, q, at(0, 1)),
            token_send(4, 0, *beside, q, at(1)),
            token_send(5, 0, *across, q, at(1)),
            token_send(6, 0, *diagonal, q, at(1)),
        ]

    def end_tokens(q):
        return [
            token_send(6, 0, *own, q, at(0, 0, mate), 1),
            token_send(7, 0, *diagonal, q, at(0, 0, mate), 1),
        ]

    def shared_tokens(q):
        return [
            token_send(0, 1, *own, q, at(2)),
            token_send(1, 1, *own, q, at(0, 1)),
            token_send(2, 1, *own, q, at(1)),
            token_send(3, 1, *beside, q, at(1)),
            token_send(4, 1, *across, q, at(1)),
            token_send(5, 1, *diagonal, q, at(1)),
        ]

    def wait_sibling_tokens(group):
        for place in (pos(1), pos(3)):
            for side in (y, 1 - y):
                for q in range(CHUNKS):
                    wait_tokens(group, place, side, q)

    total = 2 * rows
    spread_tiles = (
        lax.broadcasted_iota(jnp.int32, (LANES, total), 1) // TILE
        == lax.broadcasted_iota(jnp.int32, (LANES, total), 0)
    ).astype(jnp.bfloat16)

    def out_copy(group, h, v, side):
        return remote(
            obuf.at[group + h, v, pl.ds(side * rows, rows), :],
            out_ref.at[:, columns(y * 4 + pos(0), h)],
            osend.at[group + h, v, side],
            orecv.at[h, y, pos(0)],
            ((far if group else z) * 4 + v, side),
        )

    def attend(group, h, v):
        normed = tok[group, v, :, 0:width]
        acc = jnp.dot(normed, wbuf[h], preferred_element_type=jnp.float32)
        place = columns(pos(0), h)
        query = acc[:, 0:HD] + bias_ref[0:1, place]
        key = acc[:, HD : 2 * HD] + bias_ref[1:2, place]
        value = acc[:, 2 * HD : 3 * HD] + bias_ref[2:3, place]
        queries = rms_norm(query, qgain_ref[...])
        keys = rms_norm(key, kgain_ref[...])
        scores = lax.dot_general(
            queries, keys, (((1,), (1,)), ((), ())), preferred_element_type=jnp.float32
        ) * HD ** (-0.5)
        seen = jnp.dot(
            tok[group, v, :, width : width + LANES],
            spread_tiles,
            preferred_element_type=jnp.float32,
        )
        scores = jnp.where(seen > 0.5, scores, MASKED)
        largest = jnp.max(scores, axis=-1, keepdims=True)
        expo = jnp.exp(scores - largest)
        weights = (expo / jnp.sum(expo, axis=-1, keepdims=True)).astype(jnp.bfloat16)
        result = jnp.dot(
            weights, value.astype(jnp.bfloat16), preferred_element_type=jnp.float32
        ).astype(jnp.bfloat16)
        obuf[group + h, v] = result
        for side in range(2):
            if group:
                out_copy(group, h, v, side).start()
                continue
            away = jnp.logical_or(v != pos(0), side != y)

            @pl.when(away)
            def _():
                out_copy(group, h, v, side).start()

            @pl.when(jnp.logical_not(away))
            def _():
                out_ref[:, columns(y * 4 + pos(0), h)] = result[side * rows : (side + 1) * rows, :]

    def attend_all(group, h):
        @pl.loop(0, 4)
        def _(v):
            attend(group, h, v)

    def outs_sent(group, h):
        for v in range(4):
            for side in range(2):
                if group:
                    out_copy(group, h, v, side).wait_send()
                    continue

                @pl.when(jnp.logical_or(v != pos(0), side != y))
                def _():
                    out_copy(group, h, v, side).wait_send()

    def outs_received(h, whole):
        for flip in range(2):
            for k in range(4):
                if k or flip or whole:
                    side = 1 - y if flip else y
                    remote(
                        obuf.at[h, 0, pl.ds(0, rows), :],
                        out_ref.at[:, columns(side * 4 + pos(k), h)],
                        osend.at[h, 0, 0],
                        orecv.at[h, side, pos(k)],
                        at(1),
                    ).wait_recv()

    def z_sent(h, layer, role):
        for k in range(4):
            for way, target in ways(h, layer, role):
                z_send(h, layer * 4 + pos(k), way, target).wait_send()

    def start(copies):
        for copy in copies:
            copy.start()

    def sent(copies):
        for copy in copies:
            copy.wait_send()

    chunks = range(CHUNKS)

    def norm_and_send(first, last):
        for q in range(first, last):
            norm_chunk(q)
            start(own_tokens(q))

    def pass_direct():
        for q in chunks:
            copies = passed_tokens(q)
            wait_tokens(0, *across, q)
            copies[2].start()
            wait_tokens(0, *beside, q)
            copies[0].start()
            copies[1].start()

    norm_and_send(0, CHUNKS // 2)

    @pl.when(end)
    def _():
        own_layer(0, (2, 3), "end")
        for q in range(CHUNKS // 2):
            end_tokens(q)[0].start()

    @pl.when(inner)
    def _():
        own_layer(0, (2, 3), "inner")

    norm_and_send(CHUNKS // 2, CHUNKS)
    for k in (2, 3, 1):
        start(piece_sends(1, k))

    @pl.when(end)
    def _():
        for q in range(CHUNKS // 2, CHUNKS):
            end_tokens(q)[0].start()
        pass_direct()
        own_layer(1, range(4), "end")
        for q in chunks:
            wait_tokens(0, *diagonal, q)
            end_tokens(q)[1].start()
            passed_tokens(q)[3].start()
        relay(0, [mate], "end")
        relay(0, [3 - mate], "end")
        relay(0, [3 - z], "end")
        wait_sibling_tokens(0)
        attend_all(0, 0)
        outs_received(0, False)
        outs_received(1, True)
        outs_sent(0, 0)
        for q in chunks:
            sent(own_tokens(q) + passed_tokens(q) + end_tokens(q))
        for h in range(2):
            z_sent(h, z, "end")

    @pl.when(inner)
    def _():
        relay(0, [far, peer], "inner")
        own_layer(1, (0, 1), "inner")
        pass_direct()
        relay(0, [far_peer], "inner")
        for q in chunks:
            wait_tokens(1, *own, q)
            start(shared_tokens(q)[:3])
        own_layer(1, (2, 3), "inner")
        for q in chunks:
            wait_tokens(0, *diagonal, q)
            passed_tokens(q)[3].start()
        relay(1, [far], "inner")
        wait_sibling_tokens(0)
        attend_all(0, 0)
        for q in chunks:
            wait_tokens(1, *beside, q)
            shared_tokens(q)[3].start()
        relay(1, [peer, far_peer], "inner")
        attend_all(0, 1)
        for q in chunks:
            copies = shared_tokens(q)
            wait_tokens(1, *across, q)
            copies[4].start()
            wait_tokens(1, *diagonal, q)
            copies[5].start()
        wait_sibling_tokens(1)
        attend_all(1, 1)
        for h in range(2):
            outs_received(h, False)
            outs_sent(0, h)
        outs_sent(1, 1)
        for q in chunks:
            sent(own_tokens(q) + passed_tokens(q) + shared_tokens(q))
        for layer in (z, far, peer, far_peer):
            for h in range(2):
                z_sent(h, layer, "inner")

    for h in range(2):
        for k in (1, 2, 3):
            sent(piece_sends(h, k))


def layer_device(video, shift, scale, project_weight, project_bias, query_gain, key_gain, tile_table):
    rows, width = video.shape[1:]
    slab, columns = project_weight.shape[1:]
    tiles = rows // TILE
    table = lax.dynamic_slice_in_dim(tile_table[0], lax.axis_index("seq") * tiles, tiles, 0)
    member = jnp.any(table[:, :, None] == jnp.arange(LANES, dtype=jnp.int32), axis=1)
    member = jnp.repeat(member.astype(jnp.bfloat16), TILE, axis=0)
    vmem = pl.BlockSpec(memory_space=pltpu.VMEM)
    anywhere = pl.BlockSpec(memory_space=pl.ANY)
    dma = pltpu.SemaphoreType.DMA
    small = (video[0], shift, scale, project_bias, query_gain[None], key_gain[None])
    out = pl.pallas_call(
        layer_kernel,
        out_shape=jax.ShapeDtypeStruct((rows, 2 * columns), jnp.bfloat16),
        in_specs=[anywhere] * 3 + [vmem] + [anywhere] * 4,
        out_specs=vmem,
        scratch_shapes=[pltpu.VMEM(array.shape, array.dtype) for array in small]
        + [
            pltpu.VMEM((2, 16 * slab, 3 * HD), jnp.bfloat16),
            pltpu.VMEM((2, 4, 2 * rows, width + LANES), jnp.bfloat16),
            pltpu.VMEM((3, 4, 2 * rows, HD), jnp.bfloat16),
            dma((2,)),
            dma((6,)),
            dma((2, 3, 3)),
            dma((2, 16, 2)),
            dma((2, 16)),
            dma((2, 8, CHUNKS)),
            dma((2, 4, 2, CHUNKS)),
            dma((3, 4, 2)),
            dma((2, 2, 4)),
        ],
        compiler_params=pltpu.CompilerParams(
            collective_id=0, has_side_effects=True, vmem_limit_bytes=60 << 20
        ),
    )(*small[:3], member, *small[3:], project_weight)
    return out[None]


def solution(mesh):
    def per_device(*operands):
        video, project_weight = operands[0], operands[3]
        fits = (
            mesh.shape["dp"] == 16
            and mesh.shape["seq"] == 2
            and video.shape[0] == 1
            and project_weight.shape[2] == 8 * HD
            and video.shape[1] % (CHUNKS * TILE) == 0
            and 2 * video.shape[1] // TILE <= LANES
            and video.shape[1] <= 256
        )
        if fits:
            return layer_device(*operands)
        return gathered_device(*operands)

    return jax.shard_map(
        per_device,
        mesh=mesh,
        in_specs=(
            P("dp", "seq", None),
            P("dp", None),
            P("dp", None),
            P(None, "dp", "seq"),
            P(None, "seq"),
            P(),
            P(),
            P("dp", None, None),
        ),
        out_specs=P("dp", "seq", None),
        check_vma=False,
    )
```

```python
import jax
import jax.numpy as jnp
from jax import lax
from jax.experimental import pallas as pl
from jax.experimental.pallas import tpu as pltpu
from jax.sharding import PartitionSpec as P

HD = 128
TILE = 16


EPS = 1e-06
MASKED = -1e30
CHUNKS = 2
MESH = pl.DeviceIdType.MESH


def rms_norm(values_in, gain):
    return (
        values_in * lax.rsqrt(jnp.mean(values_in * values_in, axis=-1, keepdims=True) + EPS) * gain
    ).astype(jnp.bfloat16)


def window_attention(projected, query_gain, key_gain, table):
    seqlen = projected.shape[1]
    heads = projected.shape[2] // HD
    ntiles = seqlen // TILE
    queries = rms_norm(projected[0].reshape(seqlen, heads, HD), query_gain)
    keys = rms_norm(projected[1].reshape(seqlen, heads, HD), key_gain)
    values = projected[2].reshape(seqlen, heads, HD).astype(jnp.bfloat16)
    member = jnp.any(table[:, :, None] == jnp.arange(ntiles, dtype=table.dtype), axis=1)
    seen = jnp.repeat(jnp.repeat(member, TILE, axis=0), TILE, axis=1)
    scores = jnp.einsum(
        "qhd,khd->hqk", queries, keys, preferred_element_type=jnp.float32
    ) * HD ** (-0.5)
    scores = jnp.where(seen[None], scores, MASKED)
    largest = jnp.max(scores, axis=-1, keepdims=True)
    expo = jnp.exp(scores - largest)
    weights = (expo / jnp.sum(expo, axis=-1, keepdims=True)).astype(jnp.bfloat16)
    result = jnp.einsum("hqk,khd->qhd", weights, values, preferred_element_type=jnp.float32)
    return result.astype(jnp.bfloat16).reshape(seqlen, heads * HD)


def gathered_device(video, shift, scale, project_weight, project_bias, query_gain, key_gain, tile_table):
    tokens = video[0].astype(jnp.float32)
    centre = jnp.mean(tokens, axis=-1, keepdims=True)
    spread = jnp.mean((tokens - centre) ** 2, axis=-1, keepdims=True)
    normed = ((tokens - centre) * lax.rsqrt(spread + EPS) * (1.0 + scale[0]) + shift[0]).astype(
        jnp.bfloat16
    )
    gathered = lax.all_gather(normed, "seq", axis=0, tiled=True)
    projected = jnp.einsum(
        "sd,tdc->tsc",
        gathered,
        lax.all_gather(project_weight, "dp", axis=1, tiled=True),
        preferred_element_type=jnp.float32,
    )
    projected = projected + project_bias[:, None, :]
    local_heads = window_attention(projected, query_gain, key_gain, tile_table[0])
    returned = lax.all_to_all(local_heads, "seq", split_axis=0, concat_axis=1, tiled=True)
    return returned[None]


def layer_kernel(
    video_hbm,
    shift_hbm,
    scale_hbm,
    bias_hbm,
    qgain_hbm,
    kgain_hbm,
    table_hbm,
    weight_ref,
    out_ref,
    video_ref,
    shift_ref,
    scale_ref,
    bias_ref,
    qgain_ref,
    kgain_ref,
    table_ref,
    wbuf,
    tok,
    member,
    obuf,
    own_sem,
    small_sem,
    wsend,
    zsend,
    wrecv,
    tsend,
    trecv,
    msend,
    mrecv,
    osend,
    orecv,
):
    dp = lax.axis_index("dp")
    y = lax.axis_index("seq")
    core = lax.rem(dp, 2)
    x = lax.rem(dp // 2, 2)
    z = dp // 4
    rows, width = video_ref.shape
    slab = weight_ref.shape[1]
    end = jnp.logical_or(z == 0, z == 3)
    inner = jnp.logical_not(end)
    mate = 1 + z // 3
    far = 3 * (z // 2)
    peer = 3 - z

    def pos(k):
        xk = 1 - x if k & 2 else x
        ck = 1 - core if k & 1 else core
        return xk * 2 + ck

    def at(k, flip=0, layer=None):
        return ((z if layer is None else layer) * 4 + pos(k), 1 - y if flip else y)

    small = [
        pltpu.make_async_copy(src, dst, small_sem.at[n])
        for n, (src, dst) in enumerate(
            [
                (video_hbm, video_ref),
                (shift_hbm, shift_ref),
                (scale_hbm, scale_ref),
                (bias_hbm, bias_ref),
                (qgain_hbm, qgain_ref),
                (kgain_hbm, kgain_ref),
                (table_hbm, table_ref),
            ]
        )
    ]

    barrier = pltpu.get_barrier_semaphore()

    def greet(target):
        pl.semaphore_signal(barrier, inc=1, device_id=target, device_id_type=MESH)

    for flip in range(2):
        for k in range(4):
            if k or flip:
                greet(at(k, flip))

    @pl.when(end)
    def _():
        for flip in range(2):
            for k in range(4):
                greet(at(k, flip, mate))

    @pl.when(inner)
    def _():
        for flip in range(2):
            for k in range(4):
                greet(at(k, flip, far))
        greet(at(0, 0, peer))

    def block(h, owner):
        return wbuf.at[h, pl.ds(pl.multiple_of(owner * slab, 16), slab), :]

    def columns(place, h):
        return pl.ds(pl.multiple_of((place * 2 + h) * HD, HD), HD)

    mine = pl.ds(pl.multiple_of(dp * slab, 16), slab)

    for h in range(2):
        for i in range(3):
            pltpu.make_async_copy(
                weight_ref.at[i, :, columns(pos(0), h)],
                wbuf.at[h, mine, pl.ds(i * HD, HD)],
                own_sem.at[h],
            ).start()
        if h == 0:
            for copy in small:
                copy.start()

    @pl.when(end)
    def _():
        pl.semaphore_wait(barrier, 15)

    @pl.when(inner)
    def _():
        pl.semaphore_wait(barrier, 16)

    def remote(src, dst, send, recv, target):
        return pltpu.make_async_remote_copy(
            src_ref=src,
            dst_ref=dst,
            send_sem=send,
            recv_sem=recv,
            device_id=target,
            device_id_type=MESH,
        )

    def piece_sends(h, k):
        return [
            remote(
                weight_ref.at[i, :, columns(pos(k), h)],
                wbuf.at[h, mine, pl.ds(i * HD, HD)],
                wsend.at[h, k - 1, i],
                wrecv.at[h, dp],
                at(k),
            )
            for i in range(3)
        ]

    def z_send(h, owner, way, layer):
        return remote(
            block(h, owner),
            block(h, owner),
            zsend.at[h, owner, way],
            wrecv.at[h, owner],
            at(0, 0, layer),
        )

    def wait_block(h, owner):
        remote(
            block(h, owner), block(h, owner), zsend.at[h, owner, 0], wrecv.at[h, owner], at(1)
        ).wait_recv()

    def wait_own(h, k):
        owner = z * 4 + pos(k)
        if k:
            wait_block(h, owner)
        else:
            pltpu.make_async_copy(block(h, owner), block(h, owner), own_sem.at[h]).wait()

    def ways(h, layer, role):
        if role == "end":
            return [(0, mate)] if layer is z else []
        if layer is peer or layer is far_peer:
            return [(0, far)] if h == 0 else []
        if layer is far:
            return [(1, peer)]
        return [(1, peer), (0, far)] if h == 0 else [(1, peer)]

    far_peer = 3 - far

    def pass_on(h, layer, k, role):
        for way, target in ways(h, layer, role):
            z_send(h, layer * 4 + pos(k), way, target).start()

    def own_layer(h, ks, role):
        for k in ks:
            wait_own(h, k)
            pass_on(h, z, k, role)

    def relay(h, layers, role):
        for k in range(4):
            for layer in layers:
                wait_block(h, layer * 4 + pos(k))
                pass_on(h, layer, k, role)

    for k in (2, 3, 1):
        for copy in piece_sends(0, k):
            copy.start()

    @pl.when(end)
    def _():
        own_layer(0, (0, 1), "end")

    @pl.when(inner)
    def _():
        own_layer(0, (0, 1), "inner")

    for copy in small:
        copy.wait()
    step = 16
    part = rows // CHUNKS

    def norm_chunk(q):
        half = pl.multiple_of(y * rows + q * part, TILE)

        @pl.loop(0, part // step)
        def _(n):
            first = pl.multiple_of(n * step, step)
            tokens = video_ref[pl.ds(q * part + first, step), :].astype(jnp.float32)
            centre = jnp.mean(tokens, axis=-1, keepdims=True)
            shifted = tokens - centre
            spread = jnp.mean(shifted * shifted, axis=-1, keepdims=True)
            normed = shifted * lax.rsqrt(spread + EPS) * (1.0 + scale_ref[...]) + shift_ref[...]
            tok[0, pos(0), pl.ds(half + first, step), :] = normed.astype(jnp.bfloat16)

    def tokens_at(group, place, side, q):
        first = pl.multiple_of(side * rows + q * part, TILE)
        return tok.at[group, place, pl.ds(first, part), :]

    def token_send(n, group, place, side, q, target, to_group=None):
        to_group = group if to_group is None else to_group
        return remote(
            tokens_at(group, place, side, q),
            tokens_at(to_group, place, side, q),
            tsend.at[to_group, n, q],
            trecv.at[to_group, place, side, q],
            target,
        )

    def wait_tokens(group, place, side, q):
        token_send(0, group, place, side, q, at(1)).wait_recv()

    own, beside, across, diagonal = (
        (pos(0), y),
        (pos(2), y),
        (pos(0), 1 - y),
        (pos(2), 1 - y),
    )

    def own_tokens(q):
        return [
            token_send(0, 0, *own, q, at(2)),
            token_send(1, 0, *own, q, at(0, 1)),
            token_send(2, 0, *own, q, at(1)),
        ]

    def passed_tokens(q):
        return [
            token_send(3, 0, *beside, q, at(0, 1)),
            token_send(4, 0, *beside, q, at(1)),
            token_send(5, 0, *across, q, at(1)),
            token_send(6, 0, *diagonal, q, at(1)),
        ]

    def end_tokens(q):
        return [
            token_send(6, 0, *own, q, at(0, 0, mate), 1),
            token_send(7, 0, *diagonal, q, at(0, 0, mate), 1),
        ]

    def shared_tokens(q):
        return [
            token_send(0, 1, *own, q, at(2)),
            token_send(1, 1, *own, q, at(0, 1)),
            token_send(2, 1, *own, q, at(1)),
            token_send(3, 1, *beside, q, at(1)),
            token_send(4, 1, *across, q, at(1)),
            token_send(5, 1, *diagonal, q, at(1)),
        ]

    def wait_sibling_tokens(group):
        for place in (pos(1), pos(3)):
            for side in (y, 1 - y):
                for q in range(CHUNKS):
                    wait_tokens(group, place, side, q)

    total = 2 * rows
    slots, _, tiles = table_ref.shape

    def write_member():
        key_tile = lax.broadcasted_iota(jnp.int32, (tiles, tiles), 0)
        held = key_tile == table_ref[0]
        for n in range(1, slots):
            held = jnp.logical_or(held, key_tile == table_ref[n])
        member[0, pos(0)] = held.astype(jnp.float32).astype(jnp.bfloat16)

    def member_send(n, group, target):
        return remote(
            member.at[0, pos(0)],
            member.at[group, pos(0)],
            msend.at[n],
            mrecv.at[group, pos(0)],
            target,
        )

    def member_sends(role):
        sends = [member_send(k - 1, 0, at(k)) for k in (1, 2, 3)]
        if role == "end":
            sends += [member_send(3 + k, 1, at(k, 0, mate)) for k in range(4)]
        return sends

    def wait_members(group):
        for k in range(4):
            if k or group:
                remote(
                    member.at[group, pos(k)],
                    member.at[group, pos(k)],
                    msend.at[0],
                    mrecv.at[group, pos(k)],
                    at(1),
                ).wait_recv()

    in_tile = (
        lax.broadcasted_iota(jnp.int32, (total, tiles), 0) // TILE
        == lax.broadcasted_iota(jnp.int32, (total, tiles), 1)
    ).astype(jnp.bfloat16)

    def out_copy(group, h, v, side):
        return remote(
            obuf.at[group + h, v, pl.ds(side * rows, rows), :],
            out_ref.at[:, columns(y * 4 + pos(0), h)],
            osend.at[group + h, v, side],
            orecv.at[h, y, pos(0)],
            ((far if group else z) * 4 + v, side),
        )

    def attend(group, h, v):
        normed = tok[group, v]
        acc = jnp.dot(normed, wbuf[h], preferred_element_type=jnp.float32)
        place = columns(pos(0), h)
        query = acc[:, 0:HD] + bias_ref[0:1, place]
        key = acc[:, HD : 2 * HD] + bias_ref[1:2, place]
        value = acc[:, 2 * HD : 3 * HD] + bias_ref[2:3, place]
        queries = rms_norm(query, qgain_ref[...])
        keys = rms_norm(key, kgain_ref[...])
        scores = lax.dot_general(
            queries, keys, (((1,), (1,)), ((), ())), preferred_element_type=jnp.float32
        ) * HD ** (-0.5)
        both = (((1,), (1,)), ((), ()))
        rows_seen = lax.dot_general(
            in_tile, member[group, v], both, preferred_element_type=jnp.float32
        ).astype(jnp.bfloat16)
        seen = lax.dot_general(rows_seen, in_tile, both, preferred_element_type=jnp.float32)
        scores = jnp.where(seen > 0.5, scores, MASKED)
        largest = jnp.max(scores, axis=-1, keepdims=True)
        expo = jnp.exp(scores - largest)
        weights = (expo / jnp.sum(expo, axis=-1, keepdims=True)).astype(jnp.bfloat16)
        result = jnp.dot(
            weights, value.astype(jnp.bfloat16), preferred_element_type=jnp.float32
        ).astype(jnp.bfloat16)
        obuf[group + h, v] = result
        for side in range(2):
            if group:
                out_copy(group, h, v, side).start()
                continue
            away = jnp.logical_or(v != pos(0), side != y)

            @pl.when(away)
            def _():
                out_copy(group, h, v, side).start()

            @pl.when(jnp.logical_not(away))
            def _():
                out_ref[:, columns(y * 4 + pos(0), h)] = result[side * rows : (side + 1) * rows, :]

    def attend_all(group, h):
        @pl.loop(0, 4)
        def _(v):
            attend(group, h, v)

    def outs_sent(group, h):
        for v in range(4):
            for side in range(2):
                if group:
                    out_copy(group, h, v, side).wait_send()
                    continue

                @pl.when(jnp.logical_or(v != pos(0), side != y))
                def _():
                    out_copy(group, h, v, side).wait_send()

    def outs_received(h, whole):
        for flip in range(2):
            for k in range(4):
                if k or flip or whole:
                    side = 1 - y if flip else y
                    remote(
                        obuf.at[h, 0, pl.ds(0, rows), :],
                        out_ref.at[:, columns(side * 4 + pos(k), h)],
                        osend.at[h, 0, 0],
                        orecv.at[h, side, pos(k)],
                        at(1),
                    ).wait_recv()

    def z_sent(h, layer, role):
        for k in range(4):
            for way, target in ways(h, layer, role):
                z_send(h, layer * 4 + pos(k), way, target).wait_send()

    def start(copies):
        for copy in copies:
            copy.start()

    def sent(copies):
        for copy in copies:
            copy.wait_send()

    chunks = range(CHUNKS)

    def norm_and_send(first, last):
        for q in range(first, last):
            norm_chunk(q)
            start(own_tokens(q))

    def pass_direct():
        for q in chunks:
            copies = passed_tokens(q)
            wait_tokens(0, *across, q)
            copies[2].start()
            wait_tokens(0, *beside, q)
            copies[0].start()
            copies[1].start()

    norm_and_send(0, CHUNKS // 2)
    write_member()

    @pl.when(end)
    def _():
        start(member_sends("end"))
        own_layer(0, (2, 3), "end")
        for q in range(CHUNKS // 2):
            end_tokens(q)[0].start()

    @pl.when(inner)
    def _():
        start(member_sends("inner"))
        own_layer(0, (2, 3), "inner")

    norm_and_send(CHUNKS // 2, CHUNKS)
    for k in (2, 3, 1):
        start(piece_sends(1, k))

    @pl.when(end)
    def _():
        for q in range(CHUNKS // 2, CHUNKS):
            end_tokens(q)[0].start()
        pass_direct()
        own_layer(1, range(4), "end")
        for q in chunks:
            wait_tokens(0, *diagonal, q)
            end_tokens(q)[1].start()
            passed_tokens(q)[3].start()
        relay(0, [mate], "end")
        relay(0, [3 - mate], "end")
        relay(0, [3 - z], "end")
        wait_sibling_tokens(0)
        wait_members(0)
        attend_all(0, 0)
        outs_received(0, False)
        outs_received(1, True)
        outs_sent(0, 0)
        sent(member_sends("end"))
        for q in chunks:
            sent(own_tokens(q) + passed_tokens(q) + end_tokens(q))
        for h in range(2):
            z_sent(h, z, "end")

    @pl.when(inner)
    def _():
        relay(0, [far, peer], "inner")
        own_layer(1, (0, 1), "inner")
        pass_direct()
        relay(0, [far_peer], "inner")
        for q in chunks:
            wait_tokens(1, *own, q)
            start(shared_tokens(q)[:3])
        own_layer(1, (2, 3), "inner")
        for q in chunks:
            wait_tokens(0, *diagonal, q)
            passed_tokens(q)[3].start()
        relay(1, [far], "inner")
        wait_sibling_tokens(0)
        wait_members(0)
        attend_all(0, 0)
        for q in chunks:
            wait_tokens(1, *beside, q)
            shared_tokens(q)[3].start()
        relay(1, [peer, far_peer], "inner")
        attend_all(0, 1)
        for q in chunks:
            copies = shared_tokens(q)
            wait_tokens(1, *across, q)
            copies[4].start()
            wait_tokens(1, *diagonal, q)
            copies[5].start()
        wait_sibling_tokens(1)
        wait_members(1)
        attend_all(1, 1)
        for h in range(2):
            outs_received(h, False)
            outs_sent(0, h)
        outs_sent(1, 1)
        sent(member_sends("inner"))
        for q in chunks:
            sent(own_tokens(q) + passed_tokens(q) + shared_tokens(q))
        for layer in (z, far, peer, far_peer):
            for h in range(2):
                z_sent(h, layer, "inner")

    for h in range(2):
        for k in (1, 2, 3):
            sent(piece_sends(h, k))


def layer_device(video, shift, scale, project_weight, project_bias, query_gain, key_gain, tile_table):
    rows, width = video.shape[1:]
    slab, columns = project_weight.shape[1:]
    table = jnp.transpose(tile_table, (2, 0, 1))
    tiles = table.shape[2]
    vmem = pl.BlockSpec(memory_space=pltpu.VMEM)
    anywhere = pl.BlockSpec(memory_space=pl.ANY)
    dma = pltpu.SemaphoreType.DMA
    small = (video[0], shift, scale, project_bias, query_gain[None], key_gain[None], table)
    out = pl.pallas_call(
        layer_kernel,
        out_shape=jax.ShapeDtypeStruct((rows, 2 * columns), jnp.bfloat16),
        in_specs=[anywhere] * 8,
        out_specs=vmem,
        scratch_shapes=[pltpu.VMEM(array.shape, array.dtype) for array in small]
        + [
            pltpu.VMEM((2, 16 * slab, 3 * HD), jnp.bfloat16),
            pltpu.VMEM((2, 4, 2 * rows, width), jnp.bfloat16),
            pltpu.VMEM((2, 4, tiles, tiles), jnp.bfloat16),
            pltpu.VMEM((3, 4, 2 * rows, HD), jnp.bfloat16),
            dma((2,)),
            dma((7,)),
            dma((2, 3, 3)),
            dma((2, 16, 2)),
            dma((2, 16)),
            dma((2, 8, CHUNKS)),
            dma((2, 4, 2, CHUNKS)),
            dma((7,)),
            dma((2, 4)),
            dma((3, 4, 2)),
            dma((2, 2, 4)),
        ],
        compiler_params=pltpu.CompilerParams(
            collective_id=0, has_side_effects=True, vmem_limit_bytes=60 << 20
        ),
    )(*small, project_weight)
    return out[None]


def solution(mesh):
    def per_device(*operands):
        video, project_weight = operands[0], operands[3]
        fits = (
            mesh.shape["dp"] == 16
            and mesh.shape["seq"] == 2
            and video.shape[0] == 1
            and project_weight.shape[2] == 8 * HD
            and video.shape[1] % (CHUNKS * TILE) == 0
            and operands[7].shape[1] == 2 * video.shape[1] // TILE
            and video.shape[1] <= 256
        )
        if fits:
            return layer_device(*operands)
        return gathered_device(*operands)

    return jax.shard_map(
        per_device,
        mesh=mesh,
        in_specs=(
            P("dp", "seq", None),
            P("dp", None),
            P("dp", None),
            P(None, "dp", "seq"),
            P(None, "seq"),
            P(),
            P(),
            P("dp", None, None),
        ),
        out_specs=P("dp", "seq", None),
        check_vma=False,
    )
```

```python
import jax
import jax.numpy as jnp
from jax import lax
from jax.experimental import pallas as pl
from jax.experimental.pallas import tpu as pltpu
from jax.sharding import PartitionSpec as P

HD = 128
TILE = 16


EPS = 1e-06
MASKED = -1e30
CHUNKS = 2
MESH = pl.DeviceIdType.MESH


def rms_norm(values_in, gain):
    return (
        values_in * lax.rsqrt(jnp.mean(values_in * values_in, axis=-1, keepdims=True) + EPS) * gain
    ).astype(jnp.bfloat16)


def window_attention(projected, query_gain, key_gain, table):
    seqlen = projected.shape[1]
    heads = projected.shape[2] // HD
    ntiles = seqlen // TILE
    queries = rms_norm(projected[0].reshape(seqlen, heads, HD), query_gain)
    keys = rms_norm(projected[1].reshape(seqlen, heads, HD), key_gain)
    values = projected[2].reshape(seqlen, heads, HD).astype(jnp.bfloat16)
    member = jnp.any(table[:, :, None] == jnp.arange(ntiles, dtype=table.dtype), axis=1)
    seen = jnp.repeat(jnp.repeat(member, TILE, axis=0), TILE, axis=1)
    scores = jnp.einsum(
        "qhd,khd->hqk", queries, keys, preferred_element_type=jnp.float32
    ) * HD ** (-0.5)
    scores = jnp.where(seen[None], scores, MASKED)
    largest = jnp.max(scores, axis=-1, keepdims=True)
    expo = jnp.exp(scores - largest)
    weights = (expo / jnp.sum(expo, axis=-1, keepdims=True)).astype(jnp.bfloat16)
    result = jnp.einsum("hqk,khd->qhd", weights, values, preferred_element_type=jnp.float32)
    return result.astype(jnp.bfloat16).reshape(seqlen, heads * HD)


def gathered_device(video, shift, scale, project_weight, project_bias, query_gain, key_gain, tile_table):
    tokens = video[0].astype(jnp.float32)
    centre = jnp.mean(tokens, axis=-1, keepdims=True)
    spread = jnp.mean((tokens - centre) ** 2, axis=-1, keepdims=True)
    normed = ((tokens - centre) * lax.rsqrt(spread + EPS) * (1.0 + scale[0]) + shift[0]).astype(
        jnp.bfloat16
    )
    gathered = lax.all_gather(normed, "seq", axis=0, tiled=True)
    projected = jnp.einsum(
        "sd,tdc->tsc",
        gathered,
        lax.all_gather(project_weight, "dp", axis=1, tiled=True),
        preferred_element_type=jnp.float32,
    )
    projected = projected + project_bias[:, None, :]
    local_heads = window_attention(projected, query_gain, key_gain, tile_table[0])
    returned = lax.all_to_all(local_heads, "seq", split_axis=0, concat_axis=1, tiled=True)
    return returned[None]


def layer_kernel(
    video_hbm,
    shift_hbm,
    scale_hbm,
    bias_hbm,
    qgain_hbm,
    kgain_hbm,
    table_hbm,
    weight_ref,
    out_ref,
    video_ref,
    shift_ref,
    scale_ref,
    bias_ref,
    qgain_ref,
    kgain_ref,
    table_ref,
    wbuf,
    tok,
    member,
    obuf,
    own_sem,
    small_sem,
    wsend,
    zsend,
    wrecv,
    tsend,
    trecv,
    srecv,
    msend,
    mrecv,
    osend,
    orecv,
):
    dp = lax.axis_index("dp")
    y = lax.axis_index("seq")
    core = lax.rem(dp, 2)
    x = lax.rem(dp // 2, 2)
    z = dp // 4
    rows, width = video_ref.shape
    slab = weight_ref.shape[1]
    end = jnp.logical_or(z == 0, z == 3)
    inner = jnp.logical_not(end)
    mate = 1 + z // 3
    far = 3 * (z // 2)
    peer = 3 - z

    def pos(k):
        xk = 1 - x if k & 2 else x
        ck = 1 - core if k & 1 else core
        return xk * 2 + ck

    def at(k, flip=0, layer=None):
        return ((z if layer is None else layer) * 4 + pos(k), 1 - y if flip else y)

    small = [
        pltpu.make_async_copy(src, dst, small_sem.at[n])
        for n, (src, dst) in enumerate(
            [
                (video_hbm, video_ref),
                (shift_hbm, shift_ref),
                (scale_hbm, scale_ref),
                (bias_hbm, bias_ref),
                (qgain_hbm, qgain_ref),
                (kgain_hbm, kgain_ref),
                (table_hbm, table_ref),
            ]
        )
    ]

    barrier = pltpu.get_barrier_semaphore()

    def greet(target):
        pl.semaphore_signal(barrier, inc=1, device_id=target, device_id_type=MESH)

    for flip in range(2):
        for k in range(4):
            if k or flip:
                greet(at(k, flip))

    @pl.when(end)
    def _():
        for flip in range(2):
            for k in range(4):
                greet(at(k, flip, mate))

    @pl.when(inner)
    def _():
        for flip in range(2):
            for k in range(4):
                greet(at(k, flip, far))
        greet(at(0, 0, peer))

    def block(h, owner):
        return wbuf.at[h, pl.ds(pl.multiple_of(owner * slab, 16), slab), :]

    def columns(place, h):
        return pl.ds(pl.multiple_of((place * 2 + h) * HD, HD), HD)

    mine = pl.ds(pl.multiple_of(dp * slab, 16), slab)

    for h in range(2):
        for i in range(3):
            pltpu.make_async_copy(
                weight_ref.at[i, :, columns(pos(0), h)],
                wbuf.at[h, mine, pl.ds(i * HD, HD)],
                own_sem.at[h],
            ).start()
        if h == 0:
            for copy in small:
                copy.start()

    @pl.when(end)
    def _():
        pl.semaphore_wait(barrier, 15)

    @pl.when(inner)
    def _():
        pl.semaphore_wait(barrier, 16)

    def remote(src, dst, send, recv, target):
        return pltpu.make_async_remote_copy(
            src_ref=src,
            dst_ref=dst,
            send_sem=send,
            recv_sem=recv,
            device_id=target,
            device_id_type=MESH,
        )

    def piece_sends(h, k):
        return [
            remote(
                weight_ref.at[i, :, columns(pos(k), h)],
                wbuf.at[h, mine, pl.ds(i * HD, HD)],
                wsend.at[h, k - 1],
                wrecv.at[h, dp],
                at(k),
            )
            for i in range(3)
        ]

    def z_send(h, owner, way, layer):
        return remote(
            block(h, owner),
            block(h, owner),
            zsend.at[way],
            wrecv.at[h, owner],
            at(0, 0, layer),
        )

    def wait_block(h, owner):
        remote(
            block(h, owner), block(h, owner), zsend.at[0], wrecv.at[h, owner], at(1)
        ).wait_recv()

    def wait_own(h, k):
        owner = z * 4 + pos(k)
        if k:
            wait_block(h, owner)
        else:
            pltpu.make_async_copy(block(h, owner), block(h, owner), own_sem.at[h]).wait()

    def ways(h, layer, role):
        if role == "end":
            return [(0, mate)] if layer is z else []
        if layer is peer or layer is far_peer:
            return [(0, far)] if h == 0 else []
        if layer is far:
            return [(1, peer)]
        return [(1, peer), (0, far)] if h == 0 else [(1, peer)]

    far_peer = 3 - far

    def pass_on(h, layer, k, role):
        for way, target in ways(h, layer, role):
            z_send(h, layer * 4 + pos(k), way, target).start()

    def own_layer(h, ks, role):
        for k in ks:
            wait_own(h, k)
            pass_on(h, z, k, role)

    def relay(h, layers, role):
        for k in range(4):
            for layer in layers:
                wait_block(h, layer * 4 + pos(k))
                pass_on(h, layer, k, role)

    for k in (2, 3, 1):
        for copy in piece_sends(0, k):
            copy.start()

    @pl.when(end)
    def _():
        own_layer(0, (0, 1), "end")

    @pl.when(inner)
    def _():
        own_layer(0, (0, 1), "inner")

    for copy in small:
        copy.wait()
    step = 16
    part = rows // CHUNKS

    def norm_chunk(q):
        half = pl.multiple_of((pos(0) * 2 + y) * rows + q * part, TILE)

        @pl.loop(0, part // step)
        def _(n):
            first = pl.multiple_of(n * step, step)
            tokens = video_ref[pl.ds(q * part + first, step), :].astype(jnp.float32)
            centre = jnp.mean(tokens, axis=-1, keepdims=True)
            shifted = tokens - centre
            spread = jnp.mean(shifted * shifted, axis=-1, keepdims=True)
            normed = shifted * lax.rsqrt(spread + EPS) * (1.0 + scale_ref[...]) + shift_ref[...]
            tok[pl.ds(half + first, step), :] = normed.astype(jnp.bfloat16)

    def tokens_at(group, place, side, q):
        first = (group * 8 + place * 2 + side) * rows + q * part
        return tok.at[pl.ds(pl.multiple_of(first, TILE), part), :]

    def token_send(group, place, side, q, target, to_group=None):
        to_group = group if to_group is None else to_group
        return remote(
            tokens_at(group, place, side, q),
            tokens_at(to_group, place, side, q),
            tsend,
            trecv.at[to_group, place // 2, side, q],
            target,
        )

    def sibling_send(group, place, side, q):
        return remote(
            tokens_at(group, place, side, q),
            tokens_at(group, place, side, q),
            tsend,
            srecv.at[group, place // 2, side],
            at(1),
        )

    def wait_tokens(group, place, side, q):
        token_send(group, place, side, q, at(1)).wait_recv()

    def wait_sibling_tokens(group):
        for place in (pos(1), pos(3)):
            for side in range(2):
                first = (group * 8 + place * 2 + side) * rows
                extent = tok.at[pl.ds(pl.multiple_of(first, TILE), rows), :]
                remote(
                    extent, extent, tsend, srecv.at[group, place // 2, side], at(1)
                ).wait_recv()

    own, beside, across, diagonal = (
        (pos(0), y),
        (pos(2), y),
        (pos(0), 1 - y),
        (pos(2), 1 - y),
    )

    def own_tokens(q):
        return [
            token_send(0, *own, q, at(2)),
            token_send(0, *own, q, at(0, 1)),
            sibling_send(0, *own, q),
        ]

    def passed_tokens(q):
        return [
            token_send(0, *beside, q, at(0, 1)),
            sibling_send(0, *beside, q),
            sibling_send(0, *across, q),
            sibling_send(0, *diagonal, q),
        ]

    def end_tokens(q):
        return [
            token_send(0, *own, q, at(0, 0, mate), 1),
            token_send(0, *diagonal, q, at(0, 0, mate), 1),
        ]

    def shared_tokens(q):
        return [
            token_send(1, *own, q, at(2)),
            token_send(1, *own, q, at(0, 1)),
            sibling_send(1, *own, q),
            sibling_send(1, *beside, q),
            sibling_send(1, *across, q),
            sibling_send(1, *diagonal, q),
        ]

    total = 2 * rows
    slots, _, tiles = table_ref.shape

    def write_member():
        key_tile = lax.broadcasted_iota(jnp.int32, (tiles, tiles), 0)
        held = key_tile == table_ref[0]
        for n in range(1, slots):
            held = jnp.logical_or(held, key_tile == table_ref[n])
        member[pos(0)] = held.astype(jnp.float32).astype(jnp.bfloat16)

    def member_send(group, target):
        return remote(
            member.at[pos(0)],
            member.at[group * 4 + pos(0)],
            msend,
            mrecv.at[group],
            target,
        )

    def member_sends(role):
        sends = [member_send(0, at(k)) for k in (1, 2, 3)]
        if role == "end":
            sends += [member_send(1, at(k, 0, mate)) for k in range(4)]
        return sends

    def wait_members(group):
        extent = member.at[pl.ds(0, 3 + group)]
        remote(extent, extent, msend, mrecv.at[group], at(1)).wait_recv()

    in_tile = (
        lax.broadcasted_iota(jnp.int32, (total, tiles), 0) // TILE
        == lax.broadcasted_iota(jnp.int32, (total, tiles), 1)
    ).astype(jnp.bfloat16)

    def results_at(group, h, v, side, size):
        first = ((group + h) * 8 + v * 2 + side) * rows
        return pl.ds(pl.multiple_of(first, TILE), size)

    def out_copy(group, h, v, side):
        return remote(
            obuf.at[results_at(group, h, v, side, rows), :],
            out_ref.at[:, columns(y * 4 + pos(0), h)],
            osend,
            orecv,
            ((far if group else z) * 4 + v, side),
        )

    def attend(group, h, v):
        normed = tok[pl.ds(pl.multiple_of((group * 4 + v) * total, TILE), total), :]
        acc = jnp.dot(normed, wbuf[h], preferred_element_type=jnp.float32)
        place = columns(pos(0), h)
        query = acc[:, 0:HD] + bias_ref[0:1, place]
        key = acc[:, HD : 2 * HD] + bias_ref[1:2, place]
        value = acc[:, 2 * HD : 3 * HD] + bias_ref[2:3, place]
        queries = rms_norm(query, qgain_ref[...])
        keys = rms_norm(key, kgain_ref[...])
        scores = lax.dot_general(
            queries, keys, (((1,), (1,)), ((), ())), preferred_element_type=jnp.float32
        ) * HD ** (-0.5)
        both = (((1,), (1,)), ((), ()))
        rows_seen = lax.dot_general(
            in_tile, member[group * 4 + v], both, preferred_element_type=jnp.float32
        ).astype(jnp.bfloat16)
        seen = lax.dot_general(rows_seen, in_tile, both, preferred_element_type=jnp.float32)
        scores = jnp.where(seen > 0.5, scores, MASKED)
        largest = jnp.max(scores, axis=-1, keepdims=True)
        expo = jnp.exp(scores - largest)
        weights = (expo / jnp.sum(expo, axis=-1, keepdims=True)).astype(jnp.bfloat16)
        result = jnp.dot(
            weights, value.astype(jnp.bfloat16), preferred_element_type=jnp.float32
        ).astype(jnp.bfloat16)
        obuf[results_at(group, h, v, 0, total), :] = result
        for side in range(2):
            if group:
                out_copy(group, h, v, side).start()
                continue
            away = jnp.logical_or(v != pos(0), side != y)

            @pl.when(away)
            def _():
                out_copy(group, h, v, side).start()

            @pl.when(jnp.logical_not(away))
            def _():
                out_ref[:, columns(y * 4 + pos(0), h)] = result[side * rows : (side + 1) * rows, :]

    def attend_all(group, h):
        @pl.loop(0, 4)
        def _(v):
            attend(group, h, v)

    def bytes_sent(array, count, sem):
        extent = array.at[pl.ds(0, count)]
        remote(extent, extent, sem, sem, at(1)).wait_send()

    def all_sent(z_blocks, half_videos, members, results):
        for way, blocks in enumerate(z_blocks):
            if blocks:
                bytes_sent(wbuf.at[0], blocks * slab, zsend.at[way])
        bytes_sent(tok, half_videos * rows, tsend)
        bytes_sent(member, members, msend)
        bytes_sent(obuf, results * rows, osend)
        for h in range(2):
            for k in (1, 2, 3):
                bytes_sent(wbuf.at[0], slab, wsend.at[h, k - 1])

    def outs_received(count):
        extent = out_ref.at[:, 0 : count * HD]
        remote(extent, extent, osend, orecv, at(1)).wait_recv()

    def start(copies):
        for copy in copies:
            copy.start()

    chunks = range(CHUNKS)

    def norm_and_send(first, last):
        for q in range(first, last):
            norm_chunk(q)
            start(own_tokens(q))

    def pass_direct():
        for q in chunks:
            copies = passed_tokens(q)
            wait_tokens(0, *across, q)
            copies[2].start()
            wait_tokens(0, *beside, q)
            copies[0].start()
            copies[1].start()

    norm_and_send(0, CHUNKS // 2)
    write_member()

    @pl.when(end)
    def _():
        start(member_sends("end"))
        own_layer(0, (2, 3), "end")
        for q in range(CHUNKS // 2):
            end_tokens(q)[0].start()

    @pl.when(inner)
    def _():
        start(member_sends("inner"))
        own_layer(0, (2, 3), "inner")

    norm_and_send(CHUNKS // 2, CHUNKS)
    for k in (2, 3, 1):
        start(piece_sends(1, k))

    @pl.when(end)
    def _():
        for q in range(CHUNKS // 2, CHUNKS):
            end_tokens(q)[0].start()
        pass_direct()
        own_layer(1, range(4), "end")
        for q in chunks:
            wait_tokens(0, *diagonal, q)
            end_tokens(q)[1].start()
            passed_tokens(q)[3].start()
        relay(0, [mate], "end")
        relay(0, [3 - mate], "end")
        relay(0, [3 - z], "end")
        wait_sibling_tokens(0)
        wait_members(0)
        attend_all(0, 0)
        outs_received(15)
        all_sent((8, 0), 9, 7, 7)

    @pl.when(inner)
    def _():
        relay(0, [far, peer], "inner")
        own_layer(1, (0, 1), "inner")
        pass_direct()
        relay(0, [far_peer], "inner")
        for q in chunks:
            wait_tokens(1, *own, q)
            start(shared_tokens(q)[:3])
        own_layer(1, (2, 3), "inner")
        for q in chunks:
            wait_tokens(0, *diagonal, q)
            passed_tokens(q)[3].start()
        relay(1, [far], "inner")
        wait_sibling_tokens(0)
        wait_members(0)
        attend_all(0, 0)
        for q in chunks:
            wait_tokens(1, *beside, q)
            shared_tokens(q)[3].start()
        relay(1, [peer, far_peer], "inner")
        attend_all(0, 1)
        for q in chunks:
            copies = shared_tokens(q)
            wait_tokens(1, *across, q)
            copies[4].start()
            wait_tokens(1, *diagonal, q)
            copies[5].start()
        wait_sibling_tokens(1)
        wait_members(1)
        attend_all(1, 1)
        outs_received(14)
        all_sent((12, 16), 13, 3, 22)


def layer_device(video, shift, scale, project_weight, project_bias, query_gain, key_gain, tile_table):
    rows, width = video.shape[1:]
    slab, columns = project_weight.shape[1:]
    table = jnp.transpose(tile_table, (2, 0, 1))
    tiles = table.shape[2]
    vmem = pl.BlockSpec(memory_space=pltpu.VMEM)
    anywhere = pl.BlockSpec(memory_space=pl.ANY)
    dma = pltpu.SemaphoreType.DMA
    small = (video[0], shift, scale, project_bias, query_gain[None], key_gain[None], table)
    out = pl.pallas_call(
        layer_kernel,
        out_shape=pltpu.VMEM((rows, 2 * columns), jnp.bfloat16),
        in_specs=[anywhere] * 8,
        out_specs=vmem,
        scratch_shapes=[pltpu.VMEM(array.shape, array.dtype) for array in small]
        + [
            pltpu.VMEM((2, 16 * slab, 3 * HD), jnp.bfloat16),
            pltpu.VMEM((16 * rows, width), jnp.bfloat16),
            pltpu.VMEM((8, tiles, tiles), jnp.bfloat16),
            pltpu.VMEM((24 * rows, HD), jnp.bfloat16),
            dma((2,)),
            dma((7,)),
            dma((2, 3)),
            dma((2,)),
            dma((2, 16)),
            dma,
            dma((2, 2, 2, CHUNKS)),
            dma((2, 2, 2)),
            dma,
            dma((2,)),
            dma,
            dma,
        ],
        compiler_params=pltpu.CompilerParams(
            collective_id=0, has_side_effects=True, vmem_limit_bytes=60 << 20
        ),
    )(*small, project_weight)
    return out[None]


def solution(mesh):
    def per_device(*operands):
        video, project_weight = operands[0], operands[3]
        fits = (
            mesh.shape["dp"] == 16
            and mesh.shape["seq"] == 2
            and video.shape[0] == 1
            and project_weight.shape[2] == 8 * HD
            and video.shape[1] % (CHUNKS * TILE) == 0
            and operands[7].shape[1] == 2 * video.shape[1] // TILE
            and video.shape[1] <= 256
        )
        if fits:
            return layer_device(*operands)
        return gathered_device(*operands)

    return jax.shard_map(
        per_device,
        mesh=mesh,
        in_specs=(
            P("dp", "seq", None),
            P("dp", None),
            P("dp", None),
            P(None, "dp", "seq"),
            P(None, "seq"),
            P(),
            P(),
            P("dp", None, None),
        ),
        out_specs=P("dp", "seq", None),
        check_vma=False,
    )
```

```python
import jax
import jax.numpy as jnp
from jax import lax
from jax.experimental import pallas as pl
from jax.experimental.pallas import tpu as pltpu
from jax.sharding import PartitionSpec as P

HD = 128
TILE = 16


EPS = 1e-06
MASKED = -1e30
CHUNKS = 4
MESH = pl.DeviceIdType.MESH


def rms_norm(values_in, gain):
    return (
        values_in * lax.rsqrt(jnp.mean(values_in * values_in, axis=-1, keepdims=True) + EPS) * gain
    ).astype(jnp.bfloat16)


def window_attention(projected, query_gain, key_gain, table):
    seqlen = projected.shape[1]
    heads = projected.shape[2] // HD
    ntiles = seqlen // TILE
    queries = rms_norm(projected[0].reshape(seqlen, heads, HD), query_gain)
    keys = rms_norm(projected[1].reshape(seqlen, heads, HD), key_gain)
    values = projected[2].reshape(seqlen, heads, HD).astype(jnp.bfloat16)
    member = jnp.any(table[:, :, None] == jnp.arange(ntiles, dtype=table.dtype), axis=1)
    seen = jnp.repeat(jnp.repeat(member, TILE, axis=0), TILE, axis=1)
    scores = jnp.einsum(
        "qhd,khd->hqk", queries, keys, preferred_element_type=jnp.float32
    ) * HD ** (-0.5)
    scores = jnp.where(seen[None], scores, MASKED)
    largest = jnp.max(scores, axis=-1, keepdims=True)
    expo = jnp.exp(scores - largest)
    weights = (expo / jnp.sum(expo, axis=-1, keepdims=True)).astype(jnp.bfloat16)
    result = jnp.einsum("hqk,khd->qhd", weights, values, preferred_element_type=jnp.float32)
    return result.astype(jnp.bfloat16).reshape(seqlen, heads * HD)


def gathered_device(video, shift, scale, project_weight, project_bias, query_gain, key_gain, tile_table):
    tokens = video[0].astype(jnp.float32)
    centre = jnp.mean(tokens, axis=-1, keepdims=True)
    spread = jnp.mean((tokens - centre) ** 2, axis=-1, keepdims=True)
    normed = ((tokens - centre) * lax.rsqrt(spread + EPS) * (1.0 + scale[0]) + shift[0]).astype(
        jnp.bfloat16
    )
    gathered = lax.all_gather(normed, "seq", axis=0, tiled=True)
    projected = jnp.einsum(
        "sd,tdc->tsc",
        gathered,
        lax.all_gather(project_weight, "dp", axis=1, tiled=True),
        preferred_element_type=jnp.float32,
    )
    projected = projected + project_bias[:, None, :]
    local_heads = window_attention(projected, query_gain, key_gain, tile_table[0])
    returned = lax.all_to_all(local_heads, "seq", split_axis=0, concat_axis=1, tiled=True)
    return returned[None]


def layer_kernel(
    video_hbm,
    shift_hbm,
    scale_hbm,
    bias_hbm,
    qgain_hbm,
    kgain_hbm,
    table_hbm,
    weight_ref,
    out_ref,
    video_ref,
    shift_ref,
    scale_ref,
    bias_ref,
    qgain_ref,
    kgain_ref,
    table_ref,
    wbuf,
    tok,
    member,
    masks,
    accs,
    obuf,
    own_sem,
    small_sem,
    wsend,
    zsend,
    wrecv,
    tsend,
    trecv,
    srecv,
    msend,
    mrecv,
    osend,
    orecv,
):
    dp = lax.axis_index("dp")
    y = lax.axis_index("seq")
    core = lax.rem(dp, 2)
    x = lax.rem(dp // 2, 2)
    z = dp // 4
    rows, width = video_ref.shape
    slab = weight_ref.shape[1]
    end = jnp.logical_or(z == 0, z == 3)
    inner = jnp.logical_not(end)
    mate = 1 + z // 3
    far = 3 * (z // 2)
    peer = 3 - z

    def pos(k):
        xk = 1 - x if k & 2 else x
        ck = 1 - core if k & 1 else core
        return xk * 2 + ck

    def at(k, flip=0, layer=None):
        return ((z if layer is None else layer) * 4 + pos(k), 1 - y if flip else y)

    small = [
        pltpu.make_async_copy(src, dst, small_sem.at[n])
        for n, (src, dst) in enumerate(
            [
                (video_hbm, video_ref),
                (shift_hbm, shift_ref),
                (scale_hbm, scale_ref),
                (bias_hbm, bias_ref),
                (qgain_hbm, qgain_ref),
                (kgain_hbm, kgain_ref),
                (table_hbm, table_ref),
            ]
        )
    ]

    barrier = pltpu.get_barrier_semaphore()

    def greet(target):
        pl.semaphore_signal(barrier, inc=1, device_id=target, device_id_type=MESH)

    for flip in range(2):
        for k in range(4):
            if k or flip:
                greet(at(k, flip))

    @pl.when(end)
    def _():
        for flip in range(2):
            for k in range(4):
                greet(at(k, flip, mate))

    @pl.when(inner)
    def _():
        for flip in range(2):
            for k in range(4):
                greet(at(k, flip, far))
        greet(at(0, 0, peer))

    def block(h, owner):
        return wbuf.at[h, pl.ds(pl.multiple_of(owner * slab, 16), slab), :]

    def columns(place, h):
        return pl.ds(pl.multiple_of((place * 2 + h) * HD, HD), HD)

    mine = pl.ds(pl.multiple_of(dp * slab, 16), slab)

    for h in range(2):
        for i in range(3):
            pltpu.make_async_copy(
                weight_ref.at[i, :, columns(pos(0), h)],
                wbuf.at[h, mine, pl.ds(i * HD, HD)],
                own_sem.at[h],
            ).start()
        if h == 0:
            for copy in small:
                copy.start()

    @pl.when(end)
    def _():
        pl.semaphore_wait(barrier, 15)

    @pl.when(inner)
    def _():
        pl.semaphore_wait(barrier, 16)

    def remote(src, dst, send, recv, target):
        return pltpu.make_async_remote_copy(
            src_ref=src,
            dst_ref=dst,
            send_sem=send,
            recv_sem=recv,
            device_id=target,
            device_id_type=MESH,
        )

    def piece_sends(h, k):
        return [
            remote(
                weight_ref.at[i, :, columns(pos(k), h)],
                wbuf.at[h, mine, pl.ds(i * HD, HD)],
                wsend.at[h, k - 1],
                wrecv.at[h, dp],
                at(k),
            )
            for i in range(3)
        ]

    def z_send(h, owner, way, layer):
        return remote(
            block(h, owner),
            block(h, owner),
            zsend.at[way],
            wrecv.at[h, owner],
            at(0, 0, layer),
        )

    def wait_block(h, owner):
        remote(
            block(h, owner), block(h, owner), zsend.at[0], wrecv.at[h, owner], at(1)
        ).wait_recv()

    def wait_own(h, k):
        owner = z * 4 + pos(k)
        if k:
            wait_block(h, owner)
        else:
            pltpu.make_async_copy(block(h, owner), block(h, owner), own_sem.at[h]).wait()

    def ways(h, layer, role):
        if role == "end":
            return [(0, mate)] if layer is z else []
        if layer is peer or layer is far_peer:
            return [(0, far)] if h == 0 else []
        if layer is far:
            return [(1, peer)]
        return [(1, peer), (0, far)] if h == 0 else [(1, peer)]

    far_peer = 3 - far

    def pass_on(h, layer, k, role):
        for way, target in ways(h, layer, role):
            z_send(h, layer * 4 + pos(k), way, target).start()

    def own_layer(h, ks, role):
        for k in ks:
            wait_own(h, k)
            pass_on(h, z, k, role)

    def relay(h, layers, role):
        for k in range(4):
            for layer in layers:
                wait_block(h, layer * 4 + pos(k))
                pass_on(h, layer, k, role)

    for k in (2, 3, 1):
        for copy in piece_sends(0, k):
            copy.start()

    @pl.when(end)
    def _():
        own_layer(0, (0, 1), "end")

    @pl.when(inner)
    def _():
        own_layer(0, (0, 1), "inner")

    for copy in small:
        copy.wait()
    step = 16
    part = rows // CHUNKS

    def norm_chunk(q):
        half = pl.multiple_of((pos(0) * 2 + y) * rows + q * part, TILE)

        @pl.loop(0, part // step)
        def _(n):
            first = pl.multiple_of(n * step, step)
            tokens = video_ref[pl.ds(q * part + first, step), :].astype(jnp.float32)
            centre = jnp.mean(tokens, axis=-1, keepdims=True)
            shifted = tokens - centre
            spread = jnp.mean(shifted * shifted, axis=-1, keepdims=True)
            normed = shifted * lax.rsqrt(spread + EPS) * (1.0 + scale_ref[...]) + shift_ref[...]
            tok[pl.ds(half + first, step), :] = normed.astype(jnp.bfloat16)

    def tokens_at(group, place, side, q):
        first = (group * 8 + place * 2 + side) * rows + q * part
        return tok.at[pl.ds(pl.multiple_of(first, TILE), part), :]

    def token_send(group, place, side, q, target, to_group=None):
        to_group = group if to_group is None else to_group
        return remote(
            tokens_at(group, place, side, q),
            tokens_at(to_group, place, side, q),
            tsend,
            trecv.at[to_group, place // 2, side, q],
            target,
        )

    def sibling_send(group, place, side, q):
        return remote(
            tokens_at(group, place, side, q),
            tokens_at(group, place, side, q),
            tsend,
            srecv.at[group, place // 2, side],
            at(1),
        )

    def wait_tokens(group, place, side, q):
        token_send(group, place, side, q, at(1)).wait_recv()

    def wait_sibling_tokens(group, k, side):
        first = (group * 8 + pos(k) * 2 + side) * rows
        extent = tok.at[pl.ds(pl.multiple_of(first, TILE), rows), :]
        remote(extent, extent, tsend, srecv.at[group, pos(k) // 2, side], at(1)).wait_recv()

    own, beside, across, diagonal = (
        (pos(0), y),
        (pos(2), y),
        (pos(0), 1 - y),
        (pos(2), 1 - y),
    )

    def own_tokens(q):
        return [
            token_send(0, *own, q, at(2)),
            token_send(0, *own, q, at(0, 1)),
            sibling_send(0, *own, q),
        ]

    def passed_tokens(q):
        return [
            token_send(0, *beside, q, at(0, 1)),
            sibling_send(0, *beside, q),
            sibling_send(0, *across, q),
            sibling_send(0, *diagonal, q),
        ]

    def end_tokens(q):
        return [
            token_send(0, *own, q, at(0, 0, mate), 1),
            token_send(0, *diagonal, q, at(0, 0, mate), 1),
        ]

    def shared_tokens(q):
        return [
            token_send(1, *own, q, at(2)),
            token_send(1, *own, q, at(0, 1)),
            sibling_send(1, *own, q),
            sibling_send(1, *beside, q),
            sibling_send(1, *across, q),
            sibling_send(1, *diagonal, q),
            token_send(1, *across, q, at(2)),
        ]

    total = 2 * rows
    slots, _, tiles = table_ref.shape

    def write_member():
        key_tile = lax.broadcasted_iota(jnp.int32, (tiles, tiles), 0)
        held = key_tile == table_ref[0]
        for n in range(1, slots):
            held = jnp.logical_or(held, key_tile == table_ref[n])
        member[pos(0)] = held.astype(jnp.float32).astype(jnp.bfloat16)

    def member_send(group, target):
        return remote(
            member.at[pos(0)],
            member.at[group * 4 + pos(0)],
            msend,
            mrecv.at[group],
            target,
        )

    def member_sends(role):
        sends = [member_send(0, at(k)) for k in (1, 2, 3)]
        if role == "end":
            sends += [member_send(1, at(k, 0, mate)) for k in range(4)]
        return sends

    def wait_members(group):
        extent = member.at[pl.ds(0, 3 + group)]
        remote(extent, extent, msend, mrecv.at[group], at(1)).wait_recv()

    in_tile = (
        lax.broadcasted_iota(jnp.int32, (total, tiles), 0) // TILE
        == lax.broadcasted_iota(jnp.int32, (total, tiles), 1)
    ).astype(jnp.bfloat16)

    def results_at(group, h, v, side, size):
        first = ((group + h) * 8 + v * 2 + side) * rows
        return pl.ds(pl.multiple_of(first, TILE), size)

    def out_copy(group, h, v, side):
        return remote(
            obuf.at[results_at(group, h, v, side, rows), :],
            out_ref.at[:, columns(y * 4 + pos(0), h)],
            osend,
            orecv,
            ((far if group else z) * 4 + v, side),
        )

    both = (((1,), (1,)), ((), ()))

    def write_masks(group):
        for v in range(4):
            rows_seen = lax.dot_general(
                in_tile, member[group * 4 + v], both, preferred_element_type=jnp.float32
            ).astype(jnp.bfloat16)
            seen = lax.dot_general(rows_seen, in_tile, both, preferred_element_type=jnp.float32)
            masks[group * 4 + v] = jnp.where(seen > 0.5, 0.0, MASKED)

    most = (jnp.where(z == 1, 0, 4 * slab), 12 * slab)
    last = (far_peer * 4 * slab, 4 * slab)
    whole = (0, 16 * slab)

    def project(first, size, h, depth, add=False):
        row = pl.ds(pl.multiple_of(first, TILE), size)
        inner_rows = pl.ds(pl.multiple_of(depth[0], HD), depth[1])
        part = jnp.dot(
            tok[row, inner_rows], wbuf[h, inner_rows, :], preferred_element_type=jnp.float32
        )
        accs[row, :] = accs[row, :] + part if add else part

    def project_pair(group, h, k, depth, add=False):
        project((group * 4 + pos(k) // 2 * 2) * total, 2 * total, h, depth, add)

    def project_sides(group, h, k, side, depth, add=False):
        for m in range(2):
            video = group * 4 + pos(k) // 2 * 2 + m
            project((video * 2 + side) * rows, rows, h, depth, add)

    def attend(group, h, k):
        first = pos(k) // 2 * 2
        pair = pl.ds(pl.multiple_of((group * 4 + first) * total, TILE), 2 * total)
        acc = accs[pair, :]
        place = columns(pos(0), h)
        query = acc[:, 0:HD] + bias_ref[0:1, place]
        key = acc[:, HD : 2 * HD] + bias_ref[1:2, place]
        values = (acc[:, 2 * HD : 3 * HD] + bias_ref[2:3, place]).astype(jnp.bfloat16)
        queries = rms_norm(query, qgain_ref[...])
        keys = rms_norm(key, kgain_ref[...])
        videos = [slice(m * total, (m + 1) * total) for m in range(2)]
        scores = [
            lax.dot_general(
                queries[video], keys[video], both, preferred_element_type=jnp.float32
            ) * HD ** (-0.5)
            + masks[group * 4 + first + m]
            for m, video in enumerate(videos)
        ]
        largest = [jnp.max(one, axis=-1, keepdims=True) for one in scores]
        expo = [jnp.exp(one - top) for one, top in zip(scores, largest)]
        weights = [
            (one / jnp.sum(one, axis=-1, keepdims=True)).astype(jnp.bfloat16) for one in expo
        ]
        results = [
            jnp.dot(one, values[video], preferred_element_type=jnp.float32).astype(jnp.bfloat16)
            for one, video in zip(weights, videos)
        ]
        for m in range(2):
            obuf[results_at(group, h, first + m, 0, total), :] = results[m]
        for m in range(2):
            for side in range(2):
                copy = out_copy(group, h, first + m, side)
                if group or k:
                    copy.start()
                    continue
                away = jnp.logical_or(m != core, side != y)
                pl.when(away)(copy.start)

                @pl.when(jnp.logical_not(away))
                def _():
                    out_ref[:, columns(y * 4 + pos(0), h)] = results[m][
                        side * rows : (side + 1) * rows, :
                    ]

    def bytes_sent(array, count, sem):
        extent = array.at[pl.ds(0, count)]
        remote(extent, extent, sem, sem, at(1)).wait_send()

    def all_sent(z_blocks, token_rows, members, results):
        for way, blocks in enumerate(z_blocks):
            if blocks:
                bytes_sent(wbuf.at[0], blocks * slab, zsend.at[way])
        bytes_sent(tok, token_rows, tsend)
        bytes_sent(member, members, msend)
        bytes_sent(obuf, results * rows, osend)
        for h in range(2):
            for k in (1, 2, 3):
                bytes_sent(wbuf.at[0], slab, wsend.at[h, k - 1])

    def outs_received(count):
        extent = out_ref.at[:, 0 : count * HD]
        remote(extent, extent, osend, orecv, at(1)).wait_recv()

    def start(copies):
        for copy in copies:
            copy.start()

    chunks = range(CHUNKS)

    def norm_and_send(first, last):
        for q in range(first, last):
            norm_chunk(q)
            start(own_tokens(q))

    def pass_direct():
        for q in chunks:
            copies = passed_tokens(q)
            wait_tokens(0, *across, q)
            copies[2].start()
            wait_tokens(0, *beside, q)
            copies[0].start()
            copies[1].start()

    norm_and_send(0, CHUNKS // 2)
    write_member()

    @pl.when(end)
    def _():
        start(member_sends("end"))
        own_layer(0, (2, 3), "end")
        for q in range(CHUNKS // 2):
            end_tokens(q)[0].start()

    @pl.when(inner)
    def _():
        start(member_sends("inner"))
        own_layer(0, (2, 3), "inner")

    norm_and_send(CHUNKS // 2, CHUNKS)
    for k in (2, 3, 1):
        start(piece_sends(1, k))

    def relay_one(h, layer, k, role):
        wait_block(h, layer * 4 + pos(k))
        pass_on(h, layer, k, role)

    def pass_tokens(group, which, q):
        place, copies = {
            "beside": (beside, [shared_tokens(q)[3]]),
            "across": (across, [shared_tokens(q)[4]]),
            "diagonal": (diagonal, [(shared_tokens(q)[5] if group else passed_tokens(q)[3])]),
        }[which]
        wait_tokens(group, *place, q)
        if group and which == "across" and q == 0:
            copies = copies + [shared_tokens(q)[6]]
        start(copies)

    @pl.when(end)
    def _():
        for q in range(CHUNKS // 2, CHUNKS):
            end_tokens(q)[0].start()
        pass_direct()
        own_layer(1, range(4), "end")
        for q in (*range(1, CHUNKS), 0):
            pass_tokens(0, "diagonal", q)
            if q:
                end_tokens(q)[1].start()
        relay(0, [mate], "end")
        relay(0, [3 - mate], "end")
        relay(0, [3 - z], "end")
        wait_members(0)
        write_masks(0)
        for k in (0, 2):
            for side in range(2):
                wait_sibling_tokens(0, k + 1, side)
            project_pair(0, 0, k, whole)
            attend(0, 0, k)
        outs_received(15)
        all_sent((8, 0), (9 * CHUNKS - 1) * part, 7, 7)

    @pl.when(inner)
    def _():
        relay(0, [far, peer], "inner")
        own_layer(1, (0, 1), "inner")
        wait_members(0)
        write_masks(0)
        pass_direct()
        relay(0, [far_peer], "inner")
        for q in chunks:
            wait_tokens(1, *own, q)
            start(shared_tokens(q)[:3])
        own_layer(1, (2, 3), "inner")
        for side in range(2):
            wait_sibling_tokens(0, 1, side)
        project_pair(0, 0, 0, whole)
        attend(0, 0, 0)
        for q in chunks:
            pass_tokens(0, "diagonal", q)
        relay_one(1, far, 0, "inner")
        for side in range(2):
            wait_sibling_tokens(0, 3, side)
        project_pair(0, 0, 2, whole)
        attend(0, 0, 2)
        relay_one(1, far, 1, "inner")
        relay_one(1, far, 2, "inner")
        pass_tokens(1, "across", 0)
        relay_one(1, far, 3, "inner")
        relay(1, [peer], "inner")
        project_pair(0, 1, 0, most)
        project_pair(0, 1, 2, most)
        wait_members(1)
        write_masks(1)
        for q in chunks:
            pass_tokens(1, "beside", q)
        pass_tokens(1, "across", 1)
        wait_sibling_tokens(1, 1, y)
        project_sides(1, 1, 0, y, most)
        wait_sibling_tokens(1, 3, y)
        project_sides(1, 1, 2, y, most)
        pass_tokens(1, "across", 2)
        relay(1, [far_peer], "inner")
        project_pair(0, 1, 2, last, True)
        attend(0, 1, 2)
        project_sides(1, 1, 0, y, last, True)
        for q in range(3, CHUNKS):
            pass_tokens(1, "across", q)
        for q in (1, 2, 0):
            pass_tokens(1, "diagonal", q)
        project_sides(1, 1, 2, y, last, True)
        wait_sibling_tokens(1, 1, 1 - y)
        project_sides(1, 1, 0, 1 - y, whole)
        for q in range(3, CHUNKS):
            pass_tokens(1, "diagonal", q)
        attend(1, 1, 0)
        wait_sibling_tokens(1, 3, 1 - y)
        project_sides(1, 1, 2, 1 - y, whole)
        attend(1, 1, 2)
        project_pair(0, 1, 0, last, True)
        attend(0, 1, 0)
        outs_received(14)
        all_sent((12, 16), (13 * CHUNKS + 1) * part, 3, 22)


def layer_device(video, shift, scale, project_weight, project_bias, query_gain, key_gain, tile_table):
    rows, width = video.shape[1:]
    slab, columns = project_weight.shape[1:]
    table = jnp.transpose(tile_table, (2, 0, 1))
    tiles = table.shape[2]
    vmem = pl.BlockSpec(memory_space=pltpu.VMEM)
    anywhere = pl.BlockSpec(memory_space=pl.ANY)
    dma = pltpu.SemaphoreType.DMA
    small = (video[0], shift, scale, project_bias, query_gain[None], key_gain[None], table)
    out = pl.pallas_call(
        layer_kernel,
        out_shape=pltpu.VMEM((rows, 2 * columns), jnp.bfloat16),
        in_specs=[anywhere] * 8,
        out_specs=vmem,
        scratch_shapes=[pltpu.VMEM(array.shape, array.dtype) for array in small]
        + [
            pltpu.VMEM((2, 16 * slab, 3 * HD), jnp.bfloat16),
            pltpu.VMEM((16 * rows, width), jnp.bfloat16),
            pltpu.VMEM((8, tiles, tiles), jnp.bfloat16),
            pltpu.VMEM((8, 2 * rows, 2 * rows), jnp.float32),
            pltpu.VMEM((16 * rows, 3 * HD), jnp.float32),
            pltpu.VMEM((24 * rows, HD), jnp.bfloat16),
            dma((2,)),
            dma((7,)),
            dma((2, 3)),
            dma((2,)),
            dma((2, 16)),
            dma,
            dma((2, 2, 2, CHUNKS)),
            dma((2, 2, 2)),
            dma,
            dma((2,)),
            dma,
            dma,
        ],
        compiler_params=pltpu.CompilerParams(
            collective_id=0, has_side_effects=True, vmem_limit_bytes=60 << 20
        ),
    )(*small, project_weight)
    return out[None]


def solution(mesh):
    def per_device(*operands):
        video, project_weight = operands[0], operands[3]
        fits = (
            mesh.shape["dp"] == 16
            and mesh.shape["seq"] == 2
            and video.shape[0] == 1
            and project_weight.shape[2] == 8 * HD
            and video.shape[1] % (CHUNKS * TILE) == 0
            and operands[7].shape[1] == 2 * video.shape[1] // TILE
            and video.shape[1] <= 256
        )
        if fits:
            return layer_device(*operands)
        return gathered_device(*operands)

    return jax.shard_map(
        per_device,
        mesh=mesh,
        in_specs=(
            P("dp", "seq", None),
            P("dp", None),
            P("dp", None),
            P(None, "dp", "seq"),
            P(None, "seq"),
            P(),
            P(),
            P("dp", None, None),
        ),
        out_specs=P("dp", "seq", None),
        check_vma=False,
    )
```

```python
import jax
import jax.numpy as jnp
from jax import lax
from jax.experimental import pallas as pl
from jax.experimental.pallas import tpu as pltpu
from jax.sharding import PartitionSpec as P

HD = 128
TILE = 16


EPS = 1e-06
MASKED = -1e30
CHUNKS = (3, 2, 2, 1)
MESH = pl.DeviceIdType.MESH


def rms_norm(values_in, gain):
    return (
        values_in * lax.rsqrt(jnp.mean(values_in * values_in, axis=-1, keepdims=True) + EPS) * gain
    ).astype(jnp.bfloat16)


def window_attention(projected, query_gain, key_gain, table):
    seqlen = projected.shape[1]
    heads = projected.shape[2] // HD
    ntiles = seqlen // TILE
    queries = rms_norm(projected[0].reshape(seqlen, heads, HD), query_gain)
    keys = rms_norm(projected[1].reshape(seqlen, heads, HD), key_gain)
    values = projected[2].reshape(seqlen, heads, HD).astype(jnp.bfloat16)
    member = jnp.any(table[:, :, None] == jnp.arange(ntiles, dtype=table.dtype), axis=1)
    seen = jnp.repeat(jnp.repeat(member, TILE, axis=0), TILE, axis=1)
    scores = jnp.einsum(
        "qhd,khd->hqk", queries, keys, preferred_element_type=jnp.float32
    ) * HD ** (-0.5)
    scores = jnp.where(seen[None], scores, MASKED)
    largest = jnp.max(scores, axis=-1, keepdims=True)
    expo = jnp.exp(scores - largest)
    weights = (expo / jnp.sum(expo, axis=-1, keepdims=True)).astype(jnp.bfloat16)
    result = jnp.einsum("hqk,khd->qhd", weights, values, preferred_element_type=jnp.float32)
    return result.astype(jnp.bfloat16).reshape(seqlen, heads * HD)


def gathered_device(video, shift, scale, project_weight, project_bias, query_gain, key_gain, tile_table):
    tokens = video[0].astype(jnp.float32)
    centre = jnp.mean(tokens, axis=-1, keepdims=True)
    spread = jnp.mean((tokens - centre) ** 2, axis=-1, keepdims=True)
    normed = ((tokens - centre) * lax.rsqrt(spread + EPS) * (1.0 + scale[0]) + shift[0]).astype(
        jnp.bfloat16
    )
    gathered = lax.all_gather(normed, "seq", axis=0, tiled=True)
    projected = jnp.einsum(
        "sd,tdc->tsc",
        gathered,
        lax.all_gather(project_weight, "dp", axis=1, tiled=True),
        preferred_element_type=jnp.float32,
    )
    projected = projected + project_bias[:, None, :]
    local_heads = window_attention(projected, query_gain, key_gain, tile_table[0])
    returned = lax.all_to_all(local_heads, "seq", split_axis=0, concat_axis=1, tiled=True)
    return returned[None]


def layer_kernel(
    video_hbm,
    shift_hbm,
    scale_hbm,
    bias_hbm,
    qgain_hbm,
    kgain_hbm,
    table_hbm,
    weight_ref,
    out_ref,
    video_ref,
    shift_ref,
    scale_ref,
    bias_ref,
    qgain_ref,
    kgain_ref,
    table_ref,
    wbuf,
    tok,
    member,
    masks,
    accs,
    obuf,
    own_sem,
    small_sem,
    wsend,
    zsend,
    wrecv,
    tsend,
    trecv,
    srecv,
    msend,
    mrecv,
    osend,
    orecv,
):
    dp = lax.axis_index("dp")
    y = lax.axis_index("seq")
    core = lax.rem(dp, 2)
    x = lax.rem(dp // 2, 2)
    z = dp // 4
    rows, width = video_ref.shape
    slab = weight_ref.shape[1]
    end = jnp.logical_or(z == 0, z == 3)
    inner = jnp.logical_not(end)
    mate = 1 + z // 3
    far = 3 * (z // 2)
    peer = 3 - z

    def pos(k):
        xk = 1 - x if k & 2 else x
        ck = 1 - core if k & 1 else core
        return xk * 2 + ck

    def at(k, flip=0, layer=None):
        return ((z if layer is None else layer) * 4 + pos(k), 1 - y if flip else y)

    small = [
        pltpu.make_async_copy(src, dst, small_sem.at[n])
        for n, (src, dst) in enumerate(
            [
                (video_hbm, video_ref),
                (shift_hbm, shift_ref),
                (scale_hbm, scale_ref),
                (bias_hbm, bias_ref),
                (qgain_hbm, qgain_ref),
                (kgain_hbm, kgain_ref),
                (table_hbm, table_ref),
            ]
        )
    ]

    barrier = pltpu.get_barrier_semaphore()

    def greet(target):
        pl.semaphore_signal(barrier, inc=1, device_id=target, device_id_type=MESH)

    for flip in range(2):
        for k in range(4):
            if k or flip:
                greet(at(k, flip))

    @pl.when(end)
    def _():
        for flip in range(2):
            for k in range(4):
                greet(at(k, flip, mate))

    @pl.when(inner)
    def _():
        for flip in range(2):
            for k in range(4):
                greet(at(k, flip, far))
        greet(at(0, 0, peer))

    def block(h, owner):
        return wbuf.at[h, pl.ds(pl.multiple_of(owner * slab, 16), slab), :]

    def columns(place, h):
        return pl.ds(pl.multiple_of((place * 2 + h) * HD, HD), HD)

    mine = pl.ds(pl.multiple_of(dp * slab, 16), slab)

    for copy in small:
        copy.start()
    for h in range(2):
        for i in range(3):
            pltpu.make_async_copy(
                weight_ref.at[i, :, columns(pos(0), h)],
                wbuf.at[h, mine, pl.ds(i * HD, HD)],
                own_sem.at[h],
            ).start()

    def remote(src, dst, send, recv, target):
        return pltpu.make_async_remote_copy(
            src_ref=src,
            dst_ref=dst,
            send_sem=send,
            recv_sem=recv,
            device_id=target,
            device_id_type=MESH,
        )

    def piece_sends(h, k):
        return [
            remote(
                weight_ref.at[i, :, columns(pos(k), h)],
                wbuf.at[h, mine, pl.ds(i * HD, HD)],
                wsend.at[h, k - 1],
                wrecv.at[h, dp],
                at(k),
            )
            for i in range(3)
        ]

    def z_send(h, owner, way, layer):
        return remote(
            block(h, owner),
            block(h, owner),
            zsend.at[way],
            wrecv.at[h, owner],
            at(0, 0, layer),
        )

    def wait_block(h, owner):
        remote(
            block(h, owner), block(h, owner), zsend.at[0], wrecv.at[h, owner], at(1)
        ).wait_recv()

    def wait_own(h, k):
        owner = z * 4 + pos(k)
        if k:
            wait_block(h, owner)
        else:
            pltpu.make_async_copy(block(h, owner), block(h, owner), own_sem.at[h]).wait()

    def ways(h, layer, role):
        if role == "end":
            return [(0, mate)] if layer is z else []
        if layer is peer or layer is far_peer:
            return [(0, far)] if h == 0 else []
        if layer is far:
            return [(1, peer)]
        return [(1, peer), (0, far)] if h == 0 else [(1, peer)]

    far_peer = 3 - far

    def pass_on(h, layer, k, role):
        for way, target in ways(h, layer, role):
            z_send(h, layer * 4 + pos(k), way, target).start()

    def own_layer(h, ks, role):
        for k in ks:
            wait_own(h, k)
            pass_on(h, z, k, role)

    def relay(h, layers, role):
        for k in range(4):
            for layer in layers:
                wait_block(h, layer * 4 + pos(k))
                pass_on(h, layer, k, role)

    step = 16
    unit = rows // sum(CHUNKS)
    chunks = range(len(CHUNKS))
    offsets = [sum(CHUNKS[:q]) * unit for q in chunks]
    sizes = [count * unit for count in CHUNKS]

    def norm_chunk(q):
        half = pl.multiple_of((pos(0) * 2 + y) * rows + offsets[q], TILE)

        @pl.loop(0, sizes[q] // step)
        def _(n):
            first = pl.multiple_of(n * step, step)
            tokens = video_ref[pl.ds(offsets[q] + first, step), :].astype(jnp.float32)
            centre = jnp.mean(tokens, axis=-1, keepdims=True)
            shifted = tokens - centre
            spread = jnp.mean(shifted * shifted, axis=-1, keepdims=True)
            normed = shifted * lax.rsqrt(spread + EPS) * (1.0 + scale_ref[...]) + shift_ref[...]
            tok[pl.ds(half + first, step), :] = normed.astype(jnp.bfloat16)

    def tokens_at(group, place, side, q):
        first = (group * 8 + place * 2 + side) * rows + offsets[q]
        return tok.at[pl.ds(pl.multiple_of(first, TILE), sizes[q]), :]

    def token_send(group, place, side, q, target, to_group=None):
        to_group = group if to_group is None else to_group
        return remote(
            tokens_at(group, place, side, q),
            tokens_at(to_group, place, side, q),
            tsend,
            trecv.at[to_group, place // 2, side, q],
            target,
        )

    def sibling_send(group, place, side, q):
        return remote(
            tokens_at(group, place, side, q),
            tokens_at(group, place, side, q),
            tsend,
            srecv.at[group, place // 2, side],
            at(1),
        )

    def wait_tokens(group, place, side, q):
        token_send(group, place, side, q, at(1)).wait_recv()

    def wait_sibling_tokens(group, k, side):
        first = (group * 8 + pos(k) * 2 + side) * rows
        extent = tok.at[pl.ds(pl.multiple_of(first, TILE), rows), :]
        remote(extent, extent, tsend, srecv.at[group, pos(k) // 2, side], at(1)).wait_recv()

    own, beside, across, diagonal = (
        (pos(0), y),
        (pos(2), y),
        (pos(0), 1 - y),
        (pos(2), 1 - y),
    )

    def own_tokens(q):
        return [
            token_send(0, *own, q, at(2)),
            token_send(0, *own, q, at(0, 1)),
            sibling_send(0, *own, q),
        ]

    def passed_tokens(q):
        return [
            token_send(0, *beside, q, at(0, 1)),
            sibling_send(0, *beside, q),
            sibling_send(0, *across, q),
            sibling_send(0, *diagonal, q),
        ]

    def end_tokens(q):
        return [
            token_send(0, *own, q, at(0, 0, mate), 1),
            token_send(0, *diagonal, q, at(0, 0, mate), 1),
        ]

    def shared_tokens(q):
        return [
            token_send(1, *own, q, at(2)),
            token_send(1, *own, q, at(0, 1)),
            sibling_send(1, *own, q),
            sibling_send(1, *beside, q),
            sibling_send(1, *across, q),
            sibling_send(1, *diagonal, q),
            token_send(1, *across, q, at(2)),
        ]

    total = 2 * rows
    slots, _, tiles = table_ref.shape

    def write_member():
        key_tile = lax.broadcasted_iota(jnp.int32, (tiles, tiles), 0)
        held = key_tile == table_ref[0]
        for n in range(1, slots):
            held = jnp.logical_or(held, key_tile == table_ref[n])
        member[pos(0)] = held.astype(jnp.float32).astype(jnp.bfloat16)

    def member_send(group, target):
        return remote(
            member.at[pos(0)],
            member.at[group * 4 + pos(0)],
            msend,
            mrecv.at[group],
            target,
        )

    def member_sends(role):
        sends = [member_send(0, at(k)) for k in (1, 2, 3)]
        if role == "end":
            sends += [member_send(1, at(k, 0, mate)) for k in range(4)]
        return sends

    def wait_members(group):
        extent = member.at[pl.ds(0, 3 + group)]
        remote(extent, extent, msend, mrecv.at[group], at(1)).wait_recv()

    in_tile = (
        lax.broadcasted_iota(jnp.int32, (total, tiles), 0) // TILE
        == lax.broadcasted_iota(jnp.int32, (total, tiles), 1)
    ).astype(jnp.bfloat16)

    def results_at(group, h, v, side, size):
        first = ((group + h) * 8 + v * 2 + side) * rows
        return pl.ds(pl.multiple_of(first, TILE), size)

    def out_copy(group, h, v, side):
        return remote(
            obuf.at[results_at(group, h, v, side, rows), :],
            out_ref.at[:, columns(y * 4 + pos(0), h)],
            osend,
            orecv,
            ((far if group else z) * 4 + v, side),
        )

    both = (((1,), (1,)), ((), ()))

    def write_masks(group):
        for v in range(4):
            rows_seen = lax.dot_general(
                in_tile, member[group * 4 + v], both, preferred_element_type=jnp.float32
            ).astype(jnp.bfloat16)
            seen = lax.dot_general(rows_seen, in_tile, both, preferred_element_type=jnp.float32)
            masks[group * 4 + v] = jnp.where(seen > 0.5, 0.0, MASKED)

    most = (jnp.where(z == 1, 0, 4 * slab), 12 * slab)
    last = (far_peer * 4 * slab, 4 * slab)
    whole = (0, 16 * slab)

    def project(first, size, h, depth, add=False):
        row = pl.ds(pl.multiple_of(first, TILE), size)
        inner_rows = pl.ds(pl.multiple_of(depth[0], HD), depth[1])
        part = jnp.dot(
            tok[row, inner_rows], wbuf[h, inner_rows, :], preferred_element_type=jnp.float32
        )
        accs[row, :] = accs[row, :] + part if add else part

    def project_pair(group, h, k, depth, add=False):
        project((group * 4 + pos(k) // 2 * 2) * total, 2 * total, h, depth, add)

    def project_sides(group, h, k, side, depth, add=False):
        for m in range(2):
            video = group * 4 + pos(k) // 2 * 2 + m
            project((video * 2 + side) * rows, rows, h, depth, add)

    def attend(group, h, first, count):
        block = pl.ds(pl.multiple_of((group * 4 + first) * total, TILE), count * total)
        acc = accs[block, :]
        place = columns(pos(0), h)
        query = acc[:, 0:HD] + bias_ref[0:1, place]
        key = acc[:, HD : 2 * HD] + bias_ref[1:2, place]
        values = (acc[:, 2 * HD : 3 * HD] + bias_ref[2:3, place]).astype(jnp.bfloat16)
        queries = rms_norm(query, qgain_ref[...])
        keys = rms_norm(key, kgain_ref[...])
        videos = [slice(m * total, (m + 1) * total) for m in range(count)]
        scores = [
            lax.dot_general(
                queries[video], keys[video], both, preferred_element_type=jnp.float32
            ) * HD ** (-0.5)
            + masks[group * 4 + first + m]
            for m, video in enumerate(videos)
        ]
        largest = [jnp.max(one, axis=-1, keepdims=True) for one in scores]
        expo = [jnp.exp(one - top) for one, top in zip(scores, largest)]
        weights = [
            (one / jnp.sum(one, axis=-1, keepdims=True)).astype(jnp.bfloat16) for one in expo
        ]
        results = [
            jnp.dot(one, values[video], preferred_element_type=jnp.float32).astype(jnp.bfloat16)
            for one, video in zip(weights, videos)
        ]
        for m in range(count):
            obuf[results_at(group, h, first + m, 0, total), :] = results[m]

    def send_results(group, h, first, count, own_core=None):
        for m in range(count):
            for side in range(2):
                copy = out_copy(group, h, first + m, side)
                if own_core is None:
                    copy.start()
                    continue
                away = jnp.logical_or(m != own_core, side != y)
                pl.when(away)(copy.start)

                @pl.when(jnp.logical_not(away))
                def _():
                    out_ref[:, columns(y * 4 + pos(0), h)] = obuf[
                        results_at(group, h, first + m, side, rows), :
                    ]

    def pair(k):
        return pos(k) // 2 * 2

    def attend_pair(group, h, k, send=True):
        attend(group, h, pair(k), 2)
        if send:
            send_pair(group, h, k)

    def send_pair(group, h, k):
        send_results(group, h, pair(k), 2, None if group or k else core)

    def bytes_sent(array, count, sem):
        extent = array.at[pl.ds(0, count)]
        remote(extent, extent, sem, sem, at(1)).wait_send()

    def all_sent(z_blocks, token_rows, members, results):
        for way, blocks in enumerate(z_blocks):
            if blocks:
                bytes_sent(wbuf.at[0], blocks * slab, zsend.at[way])
        bytes_sent(tok, token_rows, tsend)
        bytes_sent(member, members, msend)
        bytes_sent(obuf, results * rows, osend)
        for h in range(2):
            for k in (1, 2, 3):
                bytes_sent(wbuf.at[0], slab, wsend.at[h, k - 1])

    def outs_received(count):
        extent = out_ref.at[:, 0 : count * HD]
        remote(extent, extent, osend, orecv, at(1)).wait_recv()

    def start(copies):
        for copy in copies:
            copy.start()

    def norm_and_send(first, last):
        for q in range(first, last):
            norm_chunk(q)
            start(own_tokens(q))

    def pass_direct():
        for q in chunks:
            copies = passed_tokens(q)
            wait_tokens(0, *across, q)
            copies[2].start()
            wait_tokens(0, *beside, q)
            copies[0].start()
            copies[1].start()

    early = len(CHUNKS) // 2
    for copy in small:
        copy.wait()
    write_member()
    for q in range(early):
        norm_chunk(q)

    @pl.when(end)
    def _():
        pl.semaphore_wait(barrier, 15)

    @pl.when(inner)
    def _():
        pl.semaphore_wait(barrier, 16)

    for k in (2, 3, 1):
        start(piece_sends(0, k))

    def first_sends(role):
        start(member_sends(role))
        for q in range(early):
            start(own_tokens(q))
        own_layer(0, (0, 1), role)

    @pl.when(end)
    def _():
        first_sends("end")

    @pl.when(inner)
    def _():
        first_sends("inner")

    norm_and_send(early, len(CHUNKS))

    @pl.when(end)
    def _():
        own_layer(0, (2, 3), "end")
        for q in chunks:
            end_tokens(q)[0].start()

    @pl.when(inner)
    def _():
        own_layer(0, (2, 3), "inner")

    for k in (2, 3, 1):
        start(piece_sends(1, k))

    def relay_one(h, layer, k, role):
        wait_block(h, layer * 4 + pos(k))
        pass_on(h, layer, k, role)

    def pass_tokens(group, which, q):
        place, copies = {
            "beside": (beside, [shared_tokens(q)[3]]),
            "across": (across, [shared_tokens(q)[4]]),
            "diagonal": (diagonal, [(shared_tokens(q)[5] if group else passed_tokens(q)[3])]),
        }[which]
        wait_tokens(group, *place, q)
        if group and which == "across" and q == 0:
            copies = copies + [shared_tokens(q)[6]]
        start(copies)

    @pl.when(end)
    def _():
        pass_direct()
        own_layer(1, range(4), "end")
        for q in (*chunks[1:], 0):
            pass_tokens(0, "diagonal", q)
            if q:
                end_tokens(q)[1].start()
        relay(0, [mate], "end")
        relay(0, [3 - mate], "end")
        relay(0, [3 - z], "end")
        wait_members(0)
        write_masks(0)
        for k in (0, 2):
            for side in range(2):
                wait_sibling_tokens(0, k + 1, side)
            project_pair(0, 0, k, whole)
            attend_pair(0, 0, k)
        outs_received(15)
        all_sent((8, 0), 9 * rows - sizes[0], 7, 7)

    @pl.when(inner)
    def _():
        relay(0, [far, peer], "inner")
        own_layer(1, (0, 1), "inner")
        pass_direct()
        wait_members(0)
        write_masks(0)
        relay(0, [far_peer], "inner")
        for q in chunks:
            wait_tokens(1, *own, q)
            start(shared_tokens(q)[:3])
        own_layer(1, (2, 3), "inner")
        for side in range(2):
            wait_sibling_tokens(0, 1, side)
        project_pair(0, 0, 0, whole)
        attend_pair(0, 0, 0)
        for q in chunks:
            pass_tokens(0, "diagonal", q)
        relay_one(1, far, 0, "inner")
        for side in range(2):
            wait_sibling_tokens(0, 3, side)
        project_pair(0, 0, 2, whole)
        attend_pair(0, 0, 2, send=False)
        relay_one(1, far, 1, "inner")
        relay_one(1, far, 2, "inner")
        pass_tokens(1, "across", 0)
        send_pair(0, 0, 2)
        relay_one(1, far, 3, "inner")
        relay(1, [peer], "inner")
        project_pair(0, 1, 0, most)
        project_pair(0, 1, 2, most)
        wait_members(1)
        write_masks(1)
        for q in chunks:
            pass_tokens(1, "beside", q)
        pass_tokens(1, "across", 1)
        wait_sibling_tokens(1, 1, y)
        project_sides(1, 1, 0, y, most)
        wait_sibling_tokens(1, 3, y)
        project_sides(1, 1, 2, y, most)
        pass_tokens(1, "across", 2)
        relay(1, [far_peer], "inner")
        project_pair(0, 1, 2, last, True)
        attend_pair(0, 1, 2)
        project_sides(1, 1, 0, y, last, True)
        for q in chunks[3:]:
            pass_tokens(1, "across", q)
        for q in (*chunks[1:], 0):
            pass_tokens(1, "diagonal", q)
        for k in range(2):
            if k:
                wait_sibling_tokens(1, 1, 1 - y)
            project(((4 + pos(k)) * 2 + 1 - y) * rows, rows, 1, whole)
            attend(1, 1, pos(k), 1)
            send_results(1, 1, pos(k), 1)
        project_sides(1, 1, 2, y, last, True)
        wait_sibling_tokens(1, 3, 1 - y)
        project_sides(1, 1, 2, 1 - y, whole)
        attend_pair(1, 1, 2)
        project_pair(0, 1, 0, last, True)
        attend_pair(0, 1, 0)
        outs_received(14)
        all_sent((12, 16), 13 * rows + sizes[0], 3, 22)


def layer_device(video, shift, scale, project_weight, project_bias, query_gain, key_gain, tile_table):
    rows, width = video.shape[1:]
    slab, columns = project_weight.shape[1:]
    table = jnp.transpose(tile_table, (2, 0, 1))
    tiles = table.shape[2]
    vmem = pl.BlockSpec(memory_space=pltpu.VMEM)
    anywhere = pl.BlockSpec(memory_space=pl.ANY)
    dma = pltpu.SemaphoreType.DMA
    small = (video[0], shift, scale, project_bias, query_gain[None], key_gain[None], table)
    out = pl.pallas_call(
        layer_kernel,
        out_shape=pltpu.VMEM((rows, 2 * columns), jnp.bfloat16),
        in_specs=[anywhere] * 8,
        out_specs=vmem,
        scratch_shapes=[pltpu.VMEM(array.shape, array.dtype) for array in small]
        + [
            pltpu.VMEM((2, 16 * slab, 3 * HD), jnp.bfloat16),
            pltpu.VMEM((16 * rows, width), jnp.bfloat16),
            pltpu.VMEM((8, tiles, tiles), jnp.bfloat16),
            pltpu.VMEM((8, 2 * rows, 2 * rows), jnp.float32),
            pltpu.VMEM((16 * rows, 3 * HD), jnp.float32),
            pltpu.VMEM((24 * rows, HD), jnp.bfloat16),
            dma((2,)),
            dma((7,)),
            dma((2, 3)),
            dma((2,)),
            dma((2, 16)),
            dma,
            dma((2, 2, 2, len(CHUNKS))),
            dma((2, 2, 2)),
            dma,
            dma((2,)),
            dma,
            dma,
        ],
        compiler_params=pltpu.CompilerParams(
            collective_id=0, has_side_effects=True, vmem_limit_bytes=60 << 20
        ),
    )(*small, project_weight)
    return out[None]


def solution(mesh):
    def per_device(*operands):
        video, project_weight = operands[0], operands[3]
        fits = (
            mesh.shape["dp"] == 16
            and mesh.shape["seq"] == 2
            and video.shape[0] == 1
            and project_weight.shape[2] == 8 * HD
            and video.shape[1] % (sum(CHUNKS) * TILE) == 0
            and operands[7].shape[1] == 2 * video.shape[1] // TILE
            and video.shape[1] <= 256
        )
        if fits:
            return layer_device(*operands)
        return gathered_device(*operands)

    return jax.shard_map(
        per_device,
        mesh=mesh,
        in_specs=(
            P("dp", "seq", None),
            P("dp", None),
            P("dp", None),
            P(None, "dp", "seq"),
            P(None, "seq"),
            P(),
            P(),
            P("dp", None, None),
        ),
        out_specs=P("dp", "seq", None),
        check_vma=False,
    )
```

```python
import jax
import jax.numpy as jnp
from jax import lax
from jax.experimental import pallas as pl
from jax.experimental.pallas import tpu as pltpu
from jax.sharding import PartitionSpec as P

HD = 128
TILE = 16


EPS = 1e-06
MASKED = -1e30
CHUNKS = (3, 2, 2, 1)
MESH = pl.DeviceIdType.MESH


def rms_norm(values_in, gain):
    return (
        values_in * lax.rsqrt(jnp.mean(values_in * values_in, axis=-1, keepdims=True) + EPS) * gain
    ).astype(jnp.bfloat16)


def window_attention(projected, query_gain, key_gain, table):
    seqlen = projected.shape[1]
    heads = projected.shape[2] // HD
    ntiles = seqlen // TILE
    queries = rms_norm(projected[0].reshape(seqlen, heads, HD), query_gain)
    keys = rms_norm(projected[1].reshape(seqlen, heads, HD), key_gain)
    values = projected[2].reshape(seqlen, heads, HD).astype(jnp.bfloat16)
    member = jnp.any(table[:, :, None] == jnp.arange(ntiles, dtype=table.dtype), axis=1)
    seen = jnp.repeat(jnp.repeat(member, TILE, axis=0), TILE, axis=1)
    scores = jnp.einsum(
        "qhd,khd->hqk", queries, keys, preferred_element_type=jnp.float32
    ) * HD ** (-0.5)
    scores = jnp.where(seen[None], scores, MASKED)
    largest = jnp.max(scores, axis=-1, keepdims=True)
    expo = jnp.exp(scores - largest)
    weights = (expo / jnp.sum(expo, axis=-1, keepdims=True)).astype(jnp.bfloat16)
    result = jnp.einsum("hqk,khd->qhd", weights, values, preferred_element_type=jnp.float32)
    return result.astype(jnp.bfloat16).reshape(seqlen, heads * HD)


def gathered_device(video, shift, scale, project_weight, project_bias, query_gain, key_gain, tile_table):
    tokens = video[0].astype(jnp.float32)
    centre = jnp.mean(tokens, axis=-1, keepdims=True)
    spread = jnp.mean((tokens - centre) ** 2, axis=-1, keepdims=True)
    normed = ((tokens - centre) * lax.rsqrt(spread + EPS) * (1.0 + scale[0]) + shift[0]).astype(
        jnp.bfloat16
    )
    gathered = lax.all_gather(normed, "seq", axis=0, tiled=True)
    projected = jnp.einsum(
        "sd,tdc->tsc",
        gathered,
        lax.all_gather(project_weight, "dp", axis=1, tiled=True),
        preferred_element_type=jnp.float32,
    )
    projected = projected + project_bias[:, None, :]
    local_heads = window_attention(projected, query_gain, key_gain, tile_table[0])
    returned = lax.all_to_all(local_heads, "seq", split_axis=0, concat_axis=1, tiled=True)
    return returned[None]


def layer_kernel(
    video_hbm,
    shift_hbm,
    scale_hbm,
    bias_hbm,
    qgain_hbm,
    kgain_hbm,
    table_hbm,
    weight_ref,
    out_ref,
    video_ref,
    shift_ref,
    scale_ref,
    bias_ref,
    qgain_ref,
    kgain_ref,
    table_ref,
    wbuf,
    tok,
    member,
    masks,
    accs,
    obuf,
    own_sem,
    small_sem,
    wsend,
    zsend,
    wrecv,
    tsend,
    trecv,
    srecv,
    msend,
    mrecv,
    osend,
    orecv,
):
    dp = lax.axis_index("dp")
    y = lax.axis_index("seq")
    core = lax.rem(dp, 2)
    x = lax.rem(dp // 2, 2)
    z = dp // 4
    rows, width = video_ref.shape
    slab = weight_ref.shape[1]
    end = jnp.logical_or(z == 0, z == 3)
    inner = jnp.logical_not(end)
    mate = 1 + z // 3
    far = 3 * (z // 2)
    peer = 3 - z

    def pos(k):
        xk = 1 - x if k & 2 else x
        ck = 1 - core if k & 1 else core
        return xk * 2 + ck

    def at(k, flip=0, layer=None):
        return ((z if layer is None else layer) * 4 + pos(k), 1 - y if flip else y)

    small = [
        pltpu.make_async_copy(src, dst, small_sem.at[n])
        for n, (src, dst) in enumerate(
            [
                (video_hbm, video_ref),
                (shift_hbm, shift_ref),
                (scale_hbm, scale_ref),
                (bias_hbm, bias_ref),
                (qgain_hbm, qgain_ref),
                (kgain_hbm, kgain_ref),
                (table_hbm, table_ref),
            ]
        )
    ]

    barrier = pltpu.get_barrier_semaphore()

    def greet(target):
        pl.semaphore_signal(barrier, inc=1, device_id=target, device_id_type=MESH)

    @pl.when(end)
    def _():
        for flip in range(2):
            for k in range(4):
                greet(at(k, flip, mate))

    @pl.when(inner)
    def _():
        for flip in range(2):
            for k in range(4):
                greet(at(k, flip, far))
        greet(at(0, 0, peer))

    for flip in range(2):
        for k in range(4):
            if k or flip:
                greet(at(k, flip))

    def half_video(group, place, side):
        return (group * 8 + place // 2 * 4 + side * 2 + lax.rem(place, 2)) * rows

    def block(h, owner):
        return wbuf.at[h, pl.ds(pl.multiple_of(owner * slab, 16), slab), :]

    def columns(place, h):
        return pl.ds(pl.multiple_of((place * 2 + h) * HD, HD), HD)

    mine = pl.ds(pl.multiple_of(dp * slab, 16), slab)

    for copy in small:
        copy.start()
    for h in range(2):
        for i in range(3):
            pltpu.make_async_copy(
                weight_ref.at[i, :, columns(pos(0), h)],
                wbuf.at[h, mine, pl.ds(i * HD, HD)],
                own_sem.at[h],
            ).start()

    def remote(src, dst, send, recv, target):
        return pltpu.make_async_remote_copy(
            src_ref=src,
            dst_ref=dst,
            send_sem=send,
            recv_sem=recv,
            device_id=target,
            device_id_type=MESH,
        )

    def piece_sends(h, k):
        return [
            remote(
                weight_ref.at[i, :, columns(pos(k), h)],
                wbuf.at[h, mine, pl.ds(i * HD, HD)],
                wsend,
                wrecv.at[h, dp],
                at(k),
            )
            for i in range(3)
        ]

    def z_send(h, owner, way, layer):
        return remote(
            block(h, owner),
            block(h, owner),
            zsend.at[way],
            wrecv.at[h, owner],
            at(0, 0, layer),
        )

    def wait_block(h, owner):
        remote(
            block(h, owner), block(h, owner), zsend.at[0], wrecv.at[h, owner], at(1)
        ).wait_recv()

    def wait_own(h, k):
        owner = z * 4 + pos(k)
        if k:
            wait_block(h, owner)
        else:
            pltpu.make_async_copy(block(h, owner), block(h, owner), own_sem.at[h]).wait()

    def ways(h, layer, role):
        if role == "end":
            return [(0, mate)] if layer is z else []
        if layer is peer or layer is far_peer:
            return [(0, far)] if h == 0 else []
        if layer is far:
            return [(1, peer)]
        return [(1, peer), (0, far)] if h == 0 else [(1, peer)]

    far_peer = 3 - far

    def pass_on(h, layer, k, role):
        for way, target in ways(h, layer, role):
            z_send(h, layer * 4 + pos(k), way, target).start()

    def own_layer(h, ks, role):
        for k in ks:
            wait_own(h, k)
            pass_on(h, z, k, role)

    def relay(h, layers, role):
        for k in range(4):
            for layer in layers:
                wait_block(h, layer * 4 + pos(k))
                pass_on(h, layer, k, role)

    step = 16
    unit = rows // sum(CHUNKS)
    chunks = range(len(CHUNKS))
    offsets = [sum(CHUNKS[:q]) * unit for q in chunks]
    sizes = [count * unit for count in CHUNKS]

    def norm_chunk(q):
        half = pl.multiple_of(half_video(0, pos(0), y) + offsets[q], TILE)

        @pl.loop(0, sizes[q] // step)
        def _(n):
            first = pl.multiple_of(n * step, step)
            tokens = video_ref[pl.ds(offsets[q] + first, step), :].astype(jnp.float32)
            centre = jnp.mean(tokens, axis=-1, keepdims=True)
            shifted = tokens - centre
            spread = jnp.mean(shifted * shifted, axis=-1, keepdims=True)
            normed = shifted * lax.rsqrt(spread + EPS) * (1.0 + scale_ref[...]) + shift_ref[...]
            tok[pl.ds(half + first, step), :] = normed.astype(jnp.bfloat16)

    def tokens_at(group, place, side, q):
        first = half_video(group, place, side) + offsets[q]
        return tok.at[pl.ds(pl.multiple_of(first, TILE), sizes[q]), :]

    def token_send(group, place, side, q, target, to_group=None):
        to_group = group if to_group is None else to_group
        return remote(
            tokens_at(group, place, side, q),
            tokens_at(to_group, place, side, q),
            tsend,
            trecv.at[to_group, place // 2, side, q],
            target,
        )

    def sibling_send(group, place, side, q):
        return remote(
            tokens_at(group, place, side, q),
            tokens_at(group, place, side, q),
            tsend,
            srecv.at[group, place // 2, side],
            at(1),
        )

    def wait_tokens(group, place, side, q):
        token_send(group, place, side, q, at(1)).wait_recv()

    def wait_sibling_tokens(group, k, side):
        first = half_video(group, pos(k), side)
        extent = tok.at[pl.ds(pl.multiple_of(first, TILE), rows), :]
        remote(extent, extent, tsend, srecv.at[group, pos(k) // 2, side], at(1)).wait_recv()

    own, beside, across, diagonal = (
        (pos(0), y),
        (pos(2), y),
        (pos(0), 1 - y),
        (pos(2), 1 - y),
    )

    def own_tokens(q):
        return [
            token_send(0, *own, q, at(2)),
            token_send(0, *own, q, at(0, 1)),
            sibling_send(0, *own, q),
        ]

    def passed_tokens(q):
        return [
            token_send(0, *beside, q, at(0, 1)),
            sibling_send(0, *beside, q),
            sibling_send(0, *across, q),
            sibling_send(0, *diagonal, q),
        ]

    def end_tokens(q):
        return [
            token_send(0, *own, q, at(0, 0, mate), 1),
            token_send(0, *diagonal, q, at(0, 0, mate), 1),
        ]

    def shared_tokens(q):
        return [
            token_send(1, *own, q, at(2)),
            token_send(1, *own, q, at(0, 1)),
            sibling_send(1, *own, q),
            sibling_send(1, *beside, q),
            sibling_send(1, *across, q),
            sibling_send(1, *diagonal, q),
            token_send(1, *across, q, at(2)),
        ]

    total = 2 * rows
    slots, _, tiles = table_ref.shape

    def write_member():
        key_tile = lax.broadcasted_iota(jnp.int32, (tiles, tiles), 0)
        held = key_tile == table_ref[0]
        for n in range(1, slots):
            held = jnp.logical_or(held, key_tile == table_ref[n])
        member[pos(0)] = held.astype(jnp.float32).astype(jnp.bfloat16)

    def member_send(group, target):
        return remote(
            member.at[pos(0)],
            member.at[group * 4 + pos(0)],
            msend,
            mrecv.at[group],
            target,
        )

    def member_sends(role):
        sends = [member_send(0, at(k)) for k in (1, 2, 3)]
        if role == "end":
            sends += [member_send(1, at(k, 0, mate)) for k in range(4)]
        return sends

    def wait_members(group):
        extent = member.at[pl.ds(0, 3 + group)]
        remote(extent, extent, msend, mrecv.at[group], at(1)).wait_recv()

    in_tile = (
        lax.broadcasted_iota(jnp.int32, (total, tiles), 0) // TILE
        == lax.broadcasted_iota(jnp.int32, (total, tiles), 1)
    ).astype(jnp.bfloat16)

    def results_at(group, h, v, side, size):
        first = ((group + h) * 8 + v * 2 + side) * rows
        return pl.ds(pl.multiple_of(first, TILE), size)

    def out_copy(group, h, v, side):
        return remote(
            obuf.at[results_at(group, h, v, side, rows), :],
            out_ref.at[:, columns(y * 4 + pos(0), h)],
            osend,
            orecv,
            ((far if group else z) * 4 + v, side),
        )

    both = (((1,), (1,)), ((), ()))

    def write_masks(group):
        for v in range(4):
            rows_seen = lax.dot_general(
                in_tile, member[group * 4 + v], both, preferred_element_type=jnp.float32
            ).astype(jnp.bfloat16)
            seen = lax.dot_general(rows_seen, in_tile, both, preferred_element_type=jnp.float32)
            masks[group * 4 + v] = jnp.where(seen > 0.5, 0.0, MASKED)

    most = (jnp.where(z == 1, 0, 2 * slab), 14 * slab)
    last = (jnp.where(z == 1, 14 * slab, 0), 2 * slab)
    whole = (0, 16 * slab)

    def project(first, size, h, depth, add=False):
        row = pl.ds(pl.multiple_of(first, TILE), size)
        inner_rows = pl.ds(pl.multiple_of(depth[0], HD), depth[1])
        part = jnp.dot(
            tok[row, inner_rows], wbuf[h, inner_rows, :], preferred_element_type=jnp.float32
        )
        accs[row, :] = accs[row, :] + part if add else part

    def project_pair(group, h, k, depth, add=False):
        project((group * 4 + pos(k) // 2 * 2) * total, 2 * total, h, depth, add)

    def project_sides(group, h, k, side, depth, add=False):
        project(half_video(group, pair(k), side), 2 * rows, h, depth, add)

    def attend(group, h, first, count):
        acc = jnp.concatenate(
            [
                accs[pl.ds(pl.multiple_of(half_video(group, first + m, side), TILE), rows), :]
                for m in range(count)
                for side in range(2)
            ]
        )
        place = columns(pos(0), h)
        query = acc[:, 0:HD] + bias_ref[0:1, place]
        key = acc[:, HD : 2 * HD] + bias_ref[1:2, place]
        values = (acc[:, 2 * HD : 3 * HD] + bias_ref[2:3, place]).astype(jnp.bfloat16)
        queries = rms_norm(query, qgain_ref[...])
        keys = rms_norm(key, kgain_ref[...])
        videos = [slice(m * total, (m + 1) * total) for m in range(count)]
        scores = [
            lax.dot_general(
                queries[video], keys[video], both, preferred_element_type=jnp.float32
            ) * HD ** (-0.5)
            + masks[group * 4 + first + m]
            for m, video in enumerate(videos)
        ]
        largest = [jnp.max(one, axis=-1, keepdims=True) for one in scores]
        expo = [jnp.exp(one - top) for one, top in zip(scores, largest)]
        weights = [
            (one / jnp.sum(one, axis=-1, keepdims=True)).astype(jnp.bfloat16) for one in expo
        ]
        results = [
            jnp.dot(one, values[video], preferred_element_type=jnp.float32).astype(jnp.bfloat16)
            for one, video in zip(weights, videos)
        ]
        for m in range(count):
            obuf[results_at(group, h, first + m, 0, total), :] = results[m]

    def send_results(group, h, first, count, own_core=None):
        for m in range(count):
            for side in range(2):
                copy = out_copy(group, h, first + m, side)
                if own_core is None:
                    copy.start()
                    continue
                away = jnp.logical_or(m != own_core, side != y)
                pl.when(away)(copy.start)

                @pl.when(jnp.logical_not(away))
                def _():
                    out_ref[:, columns(y * 4 + pos(0), h)] = obuf[
                        results_at(group, h, first + m, side, rows), :
                    ]

    def pair(k):
        return pos(k) // 2 * 2

    def attend_pair(group, h, k, send=True):
        attend(group, h, pair(k), 2)
        if send:
            send_pair(group, h, k)

    def send_pair(group, h, k):
        send_results(group, h, pair(k), 2, None if group or k else core)

    def bytes_sent(array, count, sem):
        extent = array.at[pl.ds(0, count)]
        remote(extent, extent, sem, sem, at(1)).wait_send()

    def all_sent(z_blocks, token_rows, members, results):
        for way, blocks in enumerate(z_blocks):
            if blocks:
                bytes_sent(wbuf.at[0], blocks * slab, zsend.at[way])
        bytes_sent(tok, token_rows, tsend)
        bytes_sent(member, members, msend)
        bytes_sent(obuf, results * rows, osend)
        bytes_sent(wbuf.at[0], 6 * slab, wsend)

    def outs_received(count):
        extent = out_ref.at[:, 0 : count * HD]
        remote(extent, extent, osend, orecv, at(1)).wait_recv()

    def start(copies):
        for copy in copies:
            copy.start()

    def norm_and_send(first, last):
        for q in range(first, last):
            norm_chunk(q)
            start(own_tokens(q))

    def pass_direct():
        for q in chunks:
            copies = passed_tokens(q)
            wait_tokens(0, *across, q)
            copies[2].start()
            wait_tokens(0, *beside, q)
            copies[0].start()
            copies[1].start()

    early = len(CHUNKS) // 2
    for copy in small:
        copy.wait()
    write_member()
    for q in range(early):
        norm_chunk(q)

    @pl.when(end)
    def _():
        pl.semaphore_wait(barrier, 15)

    @pl.when(inner)
    def _():
        pl.semaphore_wait(barrier, 16)

    for k in (2, 3, 1):
        start(piece_sends(0, k))

    def first_sends(role):
        start(member_sends(role))
        for q in range(early):
            start(own_tokens(q))
        own_layer(0, (0, 1), role)

    @pl.when(end)
    def _():
        first_sends("end")

    @pl.when(inner)
    def _():
        first_sends("inner")

    norm_and_send(early, len(CHUNKS))

    @pl.when(end)
    def _():
        own_layer(0, (2, 3), "end")
        for q in chunks:
            end_tokens(q)[0].start()

    @pl.when(inner)
    def _():
        own_layer(0, (2, 3), "inner")

    for k in (2, 3, 1):
        start(piece_sends(1, k))

    def first_x(layer):
        return 1 - layer // 3

    def relay_place(layer, n):
        early_x = first_x(layer)
        owner = layer * 4 + (1 - early_x if n & 2 else early_x) * 2
        owner = owner + (1 - core if n & 1 else core)
        wait_block(1, owner)
        for way, target in ways(1, layer, "inner"):
            z_send(1, owner, way, target).start()

    def pass_tokens(group, which, q):
        place, copies = {
            "beside": (beside, [shared_tokens(q)[3]]),
            "across": (across, [shared_tokens(q)[4]]),
            "diagonal": (diagonal, [(shared_tokens(q)[5] if group else passed_tokens(q)[3])]),
        }[which]
        wait_tokens(group, *place, q)
        if group and which == "across" and q == 0:
            copies = copies + [shared_tokens(q)[6]]
        start(copies)

    @pl.when(end)
    def _():
        pass_direct()
        straight = x == first_x(z)

        @pl.when(straight)
        def _():
            own_layer(1, (0, 1, 2, 3), "end")

        @pl.when(jnp.logical_not(straight))
        def _():
            own_layer(1, (2, 3, 0, 1), "end")

        for q in (*chunks[1:], 0):
            pass_tokens(0, "diagonal", q)
            if q:
                end_tokens(q)[1].start()
        relay(0, [mate], "end")
        relay(0, [3 - mate], "end")
        relay(0, [3 - z], "end")
        wait_members(0)
        write_masks(0)
        for k in (0, 2):
            for side in range(2):
                wait_sibling_tokens(0, k + 1, side)
            project_pair(0, 0, k, whole)
            attend_pair(0, 0, k)
        outs_received(15)
        all_sent((8, 0), 9 * rows - sizes[0], 7, 7)

    @pl.when(inner)
    def _():
        relay(0, [far, peer], "inner")
        own_layer(1, (0, 1), "inner")
        pass_direct()
        wait_members(0)
        write_masks(0)
        relay(0, [far_peer], "inner")
        for q in chunks:
            wait_tokens(1, *own, q)
            start(shared_tokens(q)[:3])
        own_layer(1, (2, 3), "inner")
        for side in range(2):
            wait_sibling_tokens(0, 1, side)
        project_pair(0, 0, 0, whole)
        attend_pair(0, 0, 0)
        for q in chunks:
            pass_tokens(0, "diagonal", q)
        relay_place(far, 0)
        for side in range(2):
            wait_sibling_tokens(0, 3, side)
        project_pair(0, 0, 2, whole)
        attend_pair(0, 0, 2, send=False)
        relay_place(far, 1)
        relay_place(far, 2)
        pass_tokens(1, "across", 0)
        send_pair(0, 0, 2)
        relay_place(far, 3)
        relay(1, [peer], "inner")
        wait_members(1)
        write_masks(1)
        for n in range(2):
            relay_place(far_peer, n)
        project_pair(0, 1, 0, most)
        project_pair(0, 1, 2, most)
        for q in chunks:
            pass_tokens(1, "beside", q)
        pass_tokens(1, "across", 1)
        wait_sibling_tokens(1, 1, y)
        project_sides(1, 1, 0, y, most)
        wait_sibling_tokens(1, 3, y)
        project_sides(1, 1, 2, y, most)
        pass_tokens(1, "across", 2)
        for n in range(2, 4):
            relay_place(far_peer, n)
        project_pair(0, 1, 2, last, True)
        attend_pair(0, 1, 2)
        project_sides(1, 1, 0, y, last, True)
        for q in chunks[3:]:
            pass_tokens(1, "across", q)
        for q in (*chunks[1:], 0):
            pass_tokens(1, "diagonal", q)
        for k in range(2):
            if k:
                wait_sibling_tokens(1, 1, 1 - y)
            project(half_video(1, pos(k), 1 - y), rows, 1, whole)
            attend(1, 1, pos(k), 1)
            send_results(1, 1, pos(k), 1)
        project_sides(1, 1, 2, y, last, True)
        for k in range(2, 4):
            if k == 3:
                wait_sibling_tokens(1, 3, 1 - y)
            project(half_video(1, pos(k), 1 - y), rows, 1, whole)
            attend(1, 1, pos(k), 1)
            send_results(1, 1, pos(k), 1)
        project_pair(0, 1, 0, last, True)
        attend_pair(0, 1, 0)
        outs_received(14)
        all_sent((12, 16), 13 * rows + sizes[0], 3, 22)


def layer_device(video, shift, scale, project_weight, project_bias, query_gain, key_gain, tile_table):
    rows, width = video.shape[1:]
    slab, columns = project_weight.shape[1:]
    table = jnp.transpose(tile_table, (2, 0, 1))
    tiles = table.shape[2]
    vmem = pl.BlockSpec(memory_space=pltpu.VMEM)
    anywhere = pl.BlockSpec(memory_space=pl.ANY)
    dma = pltpu.SemaphoreType.DMA
    small = (video[0], shift, scale, project_bias, query_gain[None], key_gain[None], table)
    out = pl.pallas_call(
        layer_kernel,
        out_shape=pltpu.VMEM((rows, 2 * columns), jnp.bfloat16),
        in_specs=[anywhere] * 8,
        out_specs=vmem,
        scratch_shapes=[pltpu.VMEM(array.shape, array.dtype) for array in small]
        + [
            pltpu.VMEM((2, 16 * slab, 3 * HD), jnp.bfloat16),
            pltpu.VMEM((16 * rows, width), jnp.bfloat16),
            pltpu.VMEM((8, tiles, tiles), jnp.bfloat16),
            pltpu.VMEM((8, 2 * rows, 2 * rows), jnp.float32),
            pltpu.VMEM((16 * rows, 3 * HD), jnp.float32),
            pltpu.VMEM((24 * rows, HD), jnp.bfloat16),
            dma((2,)),
            dma((7,)),
            dma,
            dma((2,)),
            dma((2, 16)),
            dma,
            dma((2, 2, 2, len(CHUNKS))),
            dma((2, 2, 2)),
            dma,
            dma((2,)),
            dma,
            dma,
        ],
        compiler_params=pltpu.CompilerParams(
            collective_id=0, has_side_effects=True, vmem_limit_bytes=60 << 20
        ),
    )(*small, project_weight)
    return out[None]


def solution(mesh):
    def per_device(*operands):
        video, project_weight = operands[0], operands[3]
        fits = (
            mesh.shape["dp"] == 16
            and mesh.shape["seq"] == 2
            and video.shape[0] == 1
            and project_weight.shape[2] == 8 * HD
            and video.shape[1] % (sum(CHUNKS) * TILE) == 0
            and operands[7].shape[1] == 2 * video.shape[1] // TILE
            and video.shape[1] <= 256
        )
        if fits:
            return layer_device(*operands)
        return gathered_device(*operands)

    return jax.shard_map(
        per_device,
        mesh=mesh,
        in_specs=(
            P("dp", "seq", None),
            P("dp", None),
            P("dp", None),
            P(None, "dp", "seq"),
            P(None, "seq"),
            P(),
            P(),
            P("dp", None, None),
        ),
        out_specs=P("dp", "seq", None),
        check_vma=False,
    )
```

```python
import jax
import jax.numpy as jnp
from jax import lax
from jax.experimental import pallas as pl
from jax.experimental.pallas import tpu as pltpu
from jax.sharding import PartitionSpec as P

HD = 128
TILE = 16


EPS = 1e-06
MASKED = -1e30
CHUNKS = (3, 2, 2, 1)
MESH = pl.DeviceIdType.MESH


def rms_norm(values_in, gain):
    return (
        values_in * lax.rsqrt(jnp.mean(values_in * values_in, axis=-1, keepdims=True) + EPS) * gain
    ).astype(jnp.bfloat16)


def window_attention(projected, query_gain, key_gain, table):
    seqlen = projected.shape[1]
    heads = projected.shape[2] // HD
    ntiles = seqlen // TILE
    queries = rms_norm(projected[0].reshape(seqlen, heads, HD), query_gain)
    keys = rms_norm(projected[1].reshape(seqlen, heads, HD), key_gain)
    values = projected[2].reshape(seqlen, heads, HD).astype(jnp.bfloat16)
    member = jnp.any(table[:, :, None] == jnp.arange(ntiles, dtype=table.dtype), axis=1)
    seen = jnp.repeat(jnp.repeat(member, TILE, axis=0), TILE, axis=1)
    scores = jnp.einsum(
        "qhd,khd->hqk", queries, keys, preferred_element_type=jnp.float32
    ) * HD ** (-0.5)
    scores = jnp.where(seen[None], scores, MASKED)
    largest = jnp.max(scores, axis=-1, keepdims=True)
    expo = jnp.exp(scores - largest)
    weights = (expo / jnp.sum(expo, axis=-1, keepdims=True)).astype(jnp.bfloat16)
    result = jnp.einsum("hqk,khd->qhd", weights, values, preferred_element_type=jnp.float32)
    return result.astype(jnp.bfloat16).reshape(seqlen, heads * HD)


def gathered_device(video, shift, scale, project_weight, project_bias, query_gain, key_gain, tile_table):
    tokens = video[0].astype(jnp.float32)
    centre = jnp.mean(tokens, axis=-1, keepdims=True)
    spread = jnp.mean((tokens - centre) ** 2, axis=-1, keepdims=True)
    normed = ((tokens - centre) * lax.rsqrt(spread + EPS) * (1.0 + scale[0]) + shift[0]).astype(
        jnp.bfloat16
    )
    gathered = lax.all_gather(normed, "seq", axis=0, tiled=True)
    projected = jnp.einsum(
        "sd,tdc->tsc",
        gathered,
        lax.all_gather(project_weight, "dp", axis=1, tiled=True),
        preferred_element_type=jnp.float32,
    )
    projected = projected + project_bias[:, None, :]
    local_heads = window_attention(projected, query_gain, key_gain, tile_table[0])
    returned = lax.all_to_all(local_heads, "seq", split_axis=0, concat_axis=1, tiled=True)
    return returned[None]


def layer_kernel(
    video_hbm,
    shift_hbm,
    scale_hbm,
    bias_hbm,
    qgain_hbm,
    kgain_hbm,
    table_hbm,
    weight_ref,
    out_ref,
    video_ref,
    shift_ref,
    scale_ref,
    bias_ref,
    qgain_ref,
    kgain_ref,
    table_ref,
    wbuf,
    tok,
    member,
    masks,
    accs,
    obuf,
    own_sem,
    small_sem,
    wsend,
    zsend,
    wrecv,
    tsend,
    trecv,
    srecv,
    msend,
    mrecv,
    osend,
    orecv,
):
    dp = lax.axis_index("dp")
    y = lax.axis_index("seq")
    core = lax.rem(dp, 2)
    x = lax.rem(dp // 2, 2)
    z = dp // 4
    rows, width = video_ref.shape
    slab = weight_ref.shape[1]
    end = jnp.logical_or(z == 0, z == 3)
    inner = jnp.logical_not(end)
    mate = 1 + z // 3
    far = 3 * (z // 2)
    peer = 3 - z

    def pos(k):
        xk = 1 - x if k & 2 else x
        ck = 1 - core if k & 1 else core
        return xk * 2 + ck

    def at(k, flip=0, layer=None):
        return ((z if layer is None else layer) * 4 + pos(k), 1 - y if flip else y)

    small = [
        pltpu.make_async_copy(src, dst, small_sem.at[n])
        for n, (src, dst) in enumerate(
            [
                (video_hbm, video_ref),
                (shift_hbm, shift_ref),
                (scale_hbm, scale_ref),
                (bias_hbm, bias_ref),
                (qgain_hbm, qgain_ref),
                (kgain_hbm, kgain_ref),
                (table_hbm, table_ref),
            ]
        )
    ]

    barrier = pltpu.get_barrier_semaphore()

    def greet(target):
        pl.semaphore_signal(barrier, inc=1, device_id=target, device_id_type=MESH)

    @pl.when(end)
    def _():
        for flip in range(2):
            for k in range(4):
                greet(at(k, flip, mate))

    @pl.when(inner)
    def _():
        for flip in range(2):
            for k in range(4):
                greet(at(k, flip, far))
        greet(at(0, 0, peer))

    for flip in range(2):
        for k in range(4):
            if k or flip:
                greet(at(k, flip))

    def half_video(group, place, side):
        return (group * 8 + place // 2 * 4 + side * 2 + lax.rem(place, 2)) * rows

    def block(h, owner):
        return wbuf.at[h, pl.ds(pl.multiple_of(owner * slab, 16), slab), :]

    def columns(place, h):
        return pl.ds(pl.multiple_of((place * 2 + h) * HD, HD), HD)

    mine = pl.ds(pl.multiple_of(dp * slab, 16), slab)

    for copy in small:
        copy.start()
    for h in range(2):
        for i in range(3):
            pltpu.make_async_copy(
                weight_ref.at[i, :, columns(pos(0), h)],
                wbuf.at[h, mine, pl.ds(i * HD, HD)],
                own_sem.at[h],
            ).start()

    def remote(src, dst, send, recv, target):
        return pltpu.make_async_remote_copy(
            src_ref=src,
            dst_ref=dst,
            send_sem=send,
            recv_sem=recv,
            device_id=target,
            device_id_type=MESH,
        )

    def piece_sends(h, k):
        return [
            remote(
                weight_ref.at[i, :, columns(pos(k), h)],
                wbuf.at[h, mine, pl.ds(i * HD, HD)],
                wsend,
                wrecv.at[h, dp],
                at(k),
            )
            for i in range(3)
        ]

    def z_send(h, owner, way, layer):
        return remote(
            block(h, owner),
            block(h, owner),
            zsend.at[way],
            wrecv.at[h, owner],
            at(0, 0, layer),
        )

    def wait_block(h, owner):
        remote(
            block(h, owner), block(h, owner), zsend.at[0], wrecv.at[h, owner], at(1)
        ).wait_recv()

    def wait_own(h, k):
        owner = z * 4 + pos(k)
        if k:
            wait_block(h, owner)
        else:
            pltpu.make_async_copy(block(h, owner), block(h, owner), own_sem.at[h]).wait()

    def ways(h, layer, role):
        if role == "end":
            return [(0, mate)] if layer is z else []
        if layer is peer or layer is far_peer:
            return [(0, far)] if h == 0 else []
        if layer is far:
            return [(1, peer)]
        return [(1, peer), (0, far)] if h == 0 else [(1, peer)]

    far_peer = 3 - far

    def pass_on(h, layer, k, role):
        for way, target in ways(h, layer, role):
            z_send(h, layer * 4 + pos(k), way, target).start()

    def own_layer(h, ks, role):
        for k in ks:
            wait_own(h, k)
            pass_on(h, z, k, role)

    def relay(h, layers, role):
        for k in range(4):
            for layer in layers:
                wait_block(h, layer * 4 + pos(k))
                pass_on(h, layer, k, role)

    step = 16
    unit = rows // sum(CHUNKS)
    chunks = range(len(CHUNKS))
    offsets = [sum(CHUNKS[:q]) * unit for q in chunks]
    sizes = [count * unit for count in CHUNKS]

    def norm_chunk(q):
        half = pl.multiple_of(half_video(0, pos(0), y) + offsets[q], TILE)

        @pl.loop(0, sizes[q] // step)
        def _(n):
            first = pl.multiple_of(n * step, step)
            tokens = video_ref[pl.ds(offsets[q] + first, step), :].astype(jnp.float32)
            centre = jnp.mean(tokens, axis=-1, keepdims=True)
            shifted = tokens - centre
            spread = jnp.mean(shifted * shifted, axis=-1, keepdims=True)
            normed = shifted * lax.rsqrt(spread + EPS) * (1.0 + scale_ref[...]) + shift_ref[...]
            tok[pl.ds(half + first, step), :] = normed.astype(jnp.bfloat16)

    def tokens_at(group, place, side, q):
        first = half_video(group, place, side) + offsets[q]
        return tok.at[pl.ds(pl.multiple_of(first, TILE), sizes[q]), :]

    def token_send(group, place, side, q, target, to_group=None):
        to_group = group if to_group is None else to_group
        return remote(
            tokens_at(group, place, side, q),
            tokens_at(to_group, place, side, q),
            tsend,
            trecv.at[to_group, place // 2, side, q],
            target,
        )

    def sibling_send(group, place, side, q):
        return remote(
            tokens_at(group, place, side, q),
            tokens_at(group, place, side, q),
            tsend,
            srecv.at[group, place // 2, side],
            at(1),
        )

    def wait_tokens(group, place, side, q):
        token_send(group, place, side, q, at(1)).wait_recv()

    def wait_sibling_tokens(group, k, side):
        first = half_video(group, pos(k), side)
        extent = tok.at[pl.ds(pl.multiple_of(first, TILE), rows), :]
        remote(extent, extent, tsend, srecv.at[group, pos(k) // 2, side], at(1)).wait_recv()

    own, beside, across, diagonal = (
        (pos(0), y),
        (pos(2), y),
        (pos(0), 1 - y),
        (pos(2), 1 - y),
    )

    def own_tokens(q):
        return [
            token_send(0, *own, q, at(2)),
            token_send(0, *own, q, at(0, 1)),
            sibling_send(0, *own, q),
        ]

    def passed_tokens(q):
        return [
            token_send(0, *beside, q, at(0, 1)),
            sibling_send(0, *beside, q),
            sibling_send(0, *across, q),
            sibling_send(0, *diagonal, q),
        ]

    def end_tokens(q):
        return [
            token_send(0, *own, q, at(0, 0, mate), 1),
            token_send(0, *diagonal, q, at(0, 0, mate), 1),
        ]

    def shared_tokens(q):
        return [
            token_send(1, *own, q, at(2)),
            token_send(1, *own, q, at(0, 1)),
            sibling_send(1, *own, q),
            sibling_send(1, *beside, q),
            sibling_send(1, *across, q),
            sibling_send(1, *diagonal, q),
            token_send(1, *across, q, at(2)),
        ]

    total = 2 * rows
    slots, _, tiles = table_ref.shape

    def write_member():
        key_tile = lax.broadcasted_iota(jnp.int32, (tiles, tiles), 0)
        held = key_tile == table_ref[0]
        for n in range(1, slots):
            held = jnp.logical_or(held, key_tile == table_ref[n])
        member[pos(0)] = held.astype(jnp.float32).astype(jnp.bfloat16)

    def member_send(group, target):
        return remote(
            member.at[pos(0)],
            member.at[group * 4 + pos(0)],
            msend,
            mrecv.at[group],
            target,
        )

    def member_sends(role):
        sends = [member_send(0, at(k)) for k in (1, 2, 3)]
        if role == "end":
            sends += [member_send(1, at(k, 0, mate)) for k in range(4)]
        return sends

    def wait_members(group):
        extent = member.at[pl.ds(0, 3 + group)]
        remote(extent, extent, msend, mrecv.at[group], at(1)).wait_recv()

    in_tile = (
        lax.broadcasted_iota(jnp.int32, (total, tiles), 0) // TILE
        == lax.broadcasted_iota(jnp.int32, (total, tiles), 1)
    ).astype(jnp.bfloat16)

    def results_at(group, h, v, side, size):
        first = ((group + h) * 8 + v * 2 + side) * rows
        return pl.ds(pl.multiple_of(first, TILE), size)

    def out_copy(group, h, v, side):
        return remote(
            obuf.at[results_at(group, h, v, side, rows), :],
            out_ref.at[:, columns(y * 4 + pos(0), h)],
            osend,
            orecv,
            ((far if group else z) * 4 + v, side),
        )

    both = (((1,), (1,)), ((), ()))

    def write_masks(group):
        for v in range(4):
            rows_seen = lax.dot_general(
                in_tile, member[group * 4 + v], both, preferred_element_type=jnp.float32
            ).astype(jnp.bfloat16)
            seen = lax.dot_general(rows_seen, in_tile, both, preferred_element_type=jnp.float32)
            masks[group * 4 + v] = jnp.where(seen > 0.5, 0.0, MASKED)

    most = (jnp.where(z == 1, 0, 2 * slab), 14 * slab)
    last = (jnp.where(z == 1, 14 * slab, 0), 2 * slab)
    whole = (0, 16 * slab)

    def project(first, size, h, depth, add=False):
        row = pl.ds(pl.multiple_of(first, TILE), size)
        inner_rows = pl.ds(pl.multiple_of(depth[0], HD), depth[1])
        part = jnp.dot(
            tok[row, inner_rows], wbuf[h, inner_rows, :], preferred_element_type=jnp.float32
        )
        accs[row, :] = accs[row, :] + part if add else part

    def project_pair(group, h, k, depth, add=False):
        project((group * 4 + pos(k) // 2 * 2) * total, 2 * total, h, depth, add)

    def project_sides(group, h, k, side, depth, add=False):
        project(half_video(group, pair(k), side), 2 * rows, h, depth, add)

    def attend(group, h, first, count):
        acc = jnp.concatenate(
            [
                accs[pl.ds(pl.multiple_of(half_video(group, first + m, side), TILE), rows), :]
                for m in range(count)
                for side in range(2)
            ]
        )
        place = columns(pos(0), h)
        query = acc[:, 0:HD] + bias_ref[0:1, place]
        key = acc[:, HD : 2 * HD] + bias_ref[1:2, place]
        values = (acc[:, 2 * HD : 3 * HD] + bias_ref[2:3, place]).astype(jnp.bfloat16)
        queries = rms_norm(query, qgain_ref[...])
        keys = rms_norm(key, kgain_ref[...])
        videos = [slice(m * total, (m + 1) * total) for m in range(count)]
        scores = [
            lax.dot_general(
                queries[video], keys[video], both, preferred_element_type=jnp.float32
            ) * HD ** (-0.5)
            + masks[group * 4 + first + m]
            for m, video in enumerate(videos)
        ]
        largest = [jnp.max(one, axis=-1, keepdims=True) for one in scores]
        expo = [jnp.exp(one - top) for one, top in zip(scores, largest)]
        weights = [
            (one / jnp.sum(one, axis=-1, keepdims=True)).astype(jnp.bfloat16) for one in expo
        ]
        results = [
            jnp.dot(one, values[video], preferred_element_type=jnp.float32).astype(jnp.bfloat16)
            for one, video in zip(weights, videos)
        ]
        for m in range(count):
            obuf[results_at(group, h, first + m, 0, total), :] = results[m]

    def send_results(group, h, first, count, own_core=None):
        for m in range(count):
            for side in range(2):
                copy = out_copy(group, h, first + m, side)
                if own_core is None:
                    copy.start()
                    continue
                away = jnp.logical_or(m != own_core, side != y)
                pl.when(away)(copy.start)

                @pl.when(jnp.logical_not(away))
                def _():
                    out_ref[:, columns(y * 4 + pos(0), h)] = obuf[
                        results_at(group, h, first + m, side, rows), :
                    ]

    def pair(k):
        return pos(k) // 2 * 2

    def attend_pair(group, h, k, send=True):
        attend(group, h, pair(k), 2)
        if send:
            send_pair(group, h, k)

    def send_pair(group, h, k):
        send_results(group, h, pair(k), 2, None if group or k else core)

    def bytes_sent(array, count, sem):
        extent = array.at[pl.ds(0, count)]
        remote(extent, extent, sem, sem, at(1)).wait_send()

    def all_sent(z_blocks, token_rows, members, results):
        for way, blocks in enumerate(z_blocks):
            if blocks:
                bytes_sent(wbuf.at[0], blocks * slab, zsend.at[way])
        bytes_sent(tok, token_rows, tsend)
        bytes_sent(member, members, msend)
        bytes_sent(obuf, results * rows, osend)
        bytes_sent(wbuf.at[0], 6 * slab, wsend)

    def outs_received(count):
        extent = out_ref.at[:, 0 : count * HD]
        remote(extent, extent, osend, orecv, at(1)).wait_recv()

    def start(copies):
        for copy in copies:
            copy.start()

    def norm_and_send(first, last):
        for q in range(first, last):
            norm_chunk(q)
            start(own_tokens(q))

    def pass_direct():
        for q in chunks:
            copies = passed_tokens(q)
            wait_tokens(0, *across, q)
            copies[2].start()
            wait_tokens(0, *beside, q)
            copies[0].start()
            copies[1].start()

    early = len(CHUNKS) // 2
    for copy in small:
        copy.wait()
    write_member()
    for q in range(early):
        norm_chunk(q)

    @pl.when(end)
    def _():
        pl.semaphore_wait(barrier, 15)

    @pl.when(inner)
    def _():
        pl.semaphore_wait(barrier, 16)

    def first_sends(role):
        own_layer(0, (0,), role)
        for k in (2, 3, 1):
            start(piece_sends(0, k))
        for q in range(early):
            start(own_tokens(q))
        start(member_sends(role))
        own_layer(0, (1,), role)

    @pl.when(end)
    def _():
        first_sends("end")

    @pl.when(inner)
    def _():
        first_sends("inner")

    norm_and_send(early, len(CHUNKS))

    @pl.when(end)
    def _():
        own_layer(0, (2, 3), "end")
        for q in chunks:
            end_tokens(q)[0].start()

    @pl.when(inner)
    def _():
        own_layer(0, (2, 3), "inner")

    for k in (2, 3, 1):
        start(piece_sends(1, k))

    def first_x(layer):
        return 1 - layer // 3

    def relay_place(layer, n):
        early_x = first_x(layer)
        owner = layer * 4 + (1 - early_x if n & 2 else early_x) * 2
        owner = owner + (1 - core if n & 1 else core)
        wait_block(1, owner)
        for way, target in ways(1, layer, "inner"):
            z_send(1, owner, way, target).start()

    def pass_tokens(group, which, q):
        place, copies = {
            "beside": (beside, [shared_tokens(q)[3]]),
            "across": (across, [shared_tokens(q)[4]]),
            "diagonal": (diagonal, [(shared_tokens(q)[5] if group else passed_tokens(q)[3])]),
        }[which]
        wait_tokens(group, *place, q)
        if group and which == "across" and q == 0:
            copies = copies + [shared_tokens(q)[6]]
        start(copies)

    @pl.when(end)
    def _():
        pass_direct()
        straight = x == first_x(z)

        @pl.when(straight)
        def _():
            own_layer(1, (0, 1, 2, 3), "end")

        @pl.when(jnp.logical_not(straight))
        def _():
            own_layer(1, (2, 3, 0, 1), "end")

        for q in (*chunks[1:], 0):
            pass_tokens(0, "diagonal", q)
            if q:
                end_tokens(q)[1].start()
        relay(0, [mate], "end")
        relay(0, [3 - mate], "end")
        relay(0, [3 - z], "end")
        wait_members(0)
        write_masks(0)
        for k in (0, 2):
            for side in range(2):
                wait_sibling_tokens(0, k + 1, side)
            project_pair(0, 0, k, whole)
            attend_pair(0, 0, k)
        outs_received(15)
        all_sent((8, 0), 9 * rows - sizes[0], 7, 7)

    @pl.when(inner)
    def _():
        relay(0, [far, peer], "inner")
        own_layer(1, (0, 1), "inner")
        pass_direct()
        wait_members(0)
        write_masks(0)
        relay(0, [far_peer], "inner")
        for q in chunks:
            wait_tokens(1, *own, q)
            start(shared_tokens(q)[:3])
        own_layer(1, (2, 3), "inner")
        for side in range(2):
            wait_sibling_tokens(0, 1, side)
        project_pair(0, 0, 0, whole)
        attend_pair(0, 0, 0)
        for q in chunks:
            pass_tokens(0, "diagonal", q)
        relay_place(far, 0)
        for side in range(2):
            wait_sibling_tokens(0, 3, side)
        project_pair(0, 0, 2, whole)
        attend_pair(0, 0, 2, send=False)
        relay_place(far, 1)
        relay_place(far, 2)
        pass_tokens(1, "across", 0)
        send_pair(0, 0, 2)
        relay_place(far, 3)
        relay(1, [peer], "inner")
        wait_members(1)
        write_masks(1)
        for n in range(2):
            relay_place(far_peer, n)
        project_pair(0, 1, 0, most)
        project_pair(0, 1, 2, most)
        for q in chunks:
            pass_tokens(1, "beside", q)
        pass_tokens(1, "across", 1)
        wait_sibling_tokens(1, 1, y)
        project_sides(1, 1, 0, y, most)
        wait_sibling_tokens(1, 3, y)
        project_sides(1, 1, 2, y, most)
        pass_tokens(1, "across", 2)
        for n in range(2, 4):
            relay_place(far_peer, n)
        project_pair(0, 1, 2, last, True)
        attend_pair(0, 1, 2)
        project_sides(1, 1, 0, y, last, True)
        for q in chunks[3:]:
            pass_tokens(1, "across", q)
        for q in (*chunks[1:], 0):
            pass_tokens(1, "diagonal", q)
        for k in range(2):
            if k:
                wait_sibling_tokens(1, 1, 1 - y)
            project(half_video(1, pos(k), 1 - y), rows, 1, whole)
            attend(1, 1, pos(k), 1)
            send_results(1, 1, pos(k), 1)
        project_sides(1, 1, 2, y, last, True)
        for k in range(2, 4):
            if k == 3:
                wait_sibling_tokens(1, 3, 1 - y)
            project(half_video(1, pos(k), 1 - y), rows, 1, whole)
            attend(1, 1, pos(k), 1)
            send_results(1, 1, pos(k), 1)
        project_pair(0, 1, 0, last, True)
        attend_pair(0, 1, 0)
        outs_received(14)
        all_sent((12, 16), 13 * rows + sizes[0], 3, 22)


def layer_device(video, shift, scale, project_weight, project_bias, query_gain, key_gain, tile_table):
    rows, width = video.shape[1:]
    slab, columns = project_weight.shape[1:]
    table = jnp.transpose(tile_table, (2, 0, 1))
    tiles = table.shape[2]
    vmem = pl.BlockSpec(memory_space=pltpu.VMEM)
    anywhere = pl.BlockSpec(memory_space=pl.ANY)
    dma = pltpu.SemaphoreType.DMA
    small = (video[0], shift, scale, project_bias, query_gain[None], key_gain[None], table)
    out = pl.pallas_call(
        layer_kernel,
        out_shape=pltpu.VMEM((rows, 2 * columns), jnp.bfloat16),
        in_specs=[anywhere] * 8,
        out_specs=vmem,
        scratch_shapes=[pltpu.VMEM(array.shape, array.dtype) for array in small]
        + [
            pltpu.VMEM((2, 16 * slab, 3 * HD), jnp.bfloat16),
            pltpu.VMEM((16 * rows, width), jnp.bfloat16),
            pltpu.VMEM((8, tiles, tiles), jnp.bfloat16),
            pltpu.VMEM((8, 2 * rows, 2 * rows), jnp.float32),
            pltpu.VMEM((16 * rows, 3 * HD), jnp.float32),
            pltpu.VMEM((24 * rows, HD), jnp.bfloat16),
            dma((2,)),
            dma((7,)),
            dma,
            dma((2,)),
            dma((2, 16)),
            dma,
            dma((2, 2, 2, len(CHUNKS))),
            dma((2, 2, 2)),
            dma,
            dma((2,)),
            dma,
            dma,
        ],
        compiler_params=pltpu.CompilerParams(
            collective_id=0, has_side_effects=True, vmem_limit_bytes=60 << 20
        ),
    )(*small, project_weight)
    return out[None]


def solution(mesh):
    def per_device(*operands):
        video, project_weight = operands[0], operands[3]
        fits = (
            mesh.shape["dp"] == 16
            and mesh.shape["seq"] == 2
            and video.shape[0] == 1
            and project_weight.shape[2] == 8 * HD
            and video.shape[1] % (sum(CHUNKS) * TILE) == 0
            and operands[7].shape[1] == 2 * video.shape[1] // TILE
            and video.shape[1] <= 256
        )
        if fits:
            return layer_device(*operands)
        return gathered_device(*operands)

    return jax.shard_map(
        per_device,
        mesh=mesh,
        in_specs=(
            P("dp", "seq", None),
            P("dp", None),
            P("dp", None),
            P(None, "dp", "seq"),
            P(None, "seq"),
            P(),
            P(),
            P("dp", None, None),
        ),
        out_specs=P("dp", "seq", None),
        check_vma=False,
    )
```
